512 devices in a mesh: outer: 4 (over x), inner: 128 (over z, y, core).
Axes of the slice: x: 4, y: 8, z: 8, core: 2. Of those that a mesh axis runs over, the one named last changes fastest.
Arguments:
- acts: bfloat16 [512, 2, 512, 512], P(('outer', 'inner')), may hold values from -6 to 6
- cotangent: bfloat16 [512, 2, 512, 512], P(('outer', 'inner')), may hold values from -6 to 6
- residual: float32 [512, 2048, 128], P(('outer', 'inner')), may hold values from -0.6 to 0.6
- owner_residual: float32 [512, 16, 128], P(('outer', 'inner')), may hold values from -3 to 3
- in_count: int32 [512, 2, 128], P(('outer', 'inner')), may hold values from 1 to 8, as said below
- in_rank: int32 [512, 2, 2048], P(('outer', 'inner')), may hold values from 0 to 15, as said below
- out_count: int32 [512, 2], P(('outer', 'inner')), may hold values from 1 to 8
- out_rank: int32 [512, 2, 16], P(('outer', 'inner')), may hold values from 0 to 15, as said below
Outputs:
- applied: bfloat16 [512, 512], replicated
- new_residual: float32 [512, 2048, 128], P(('outer', 'inner'))
- new_owner_residual: float32 [512, 16, 128], P(('outer', 'inner'))
The draws below stay inside these ranges and needn't reach their ends.
Inputs may be any that keep to these rules, and one draw needn't show every extreme that they name: `in_count`: each step has one owner that receives 8 blocks from every replica. `in_rank`: for each replica, step and owner, the ranks of that owner's 16 blocks are a permutation of 0 to 15. `out_rank`: for each replica and step a permutation of 0 to 15.
All inputs are finite; a program needn't handle non-finite values.
Results may differ from the reference program's by a relative error of at most 0.0065.
Values may be sent and summed in bfloat16 or wider, within the bound.
No kernel may reach another device: no remote copies, remote signals or barrier semaphores. Data moves between devices by JAX's collectives and lax.ppermute only.
A program may use at most 64 MiB of HBM per device.

```python
import math
import jax
import jax.numpy as jnp
from jax import lax

TILE_R = 512
TILE_C = 512
BLOCK = 128
STEPS = 2
TOK = 512
REPLICAS = 512
BLOCKS = 2048
REGION = 16
CAP = 8
N_OUTER = 4
N_INNER = 128


def skewed_counts(key, shape):
    first = jax.random.randint(jax.random.fold_in(key, 1), shape, 0, CAP)
    second = jax.random.randint(jax.random.fold_in(key, 2), shape, 0, CAP)
    return jnp.minimum(first, second) + 1


def draw_in_count(key, part):
    counts = skewed_counts(jax.random.fold_in(key, 11), (REPLICAS, STEPS, N_INNER))
    hottest = jax.random.randint(jax.random.fold_in(key, 5), (STEPS,), 0, N_INNER)
    owners = jnp.arange(N_INNER)[None, None, :]
    return jnp.where(owners == hottest[None, :, None], CAP, counts).astype(jnp.int32)


def permutations(key, count):
    keys = jax.random.split(key, count)
    return jax.vmap(lambda single: jax.random.permutation(single, REGION))(keys)


def draw_in_rank(key, part):
    ranks = permutations(jax.random.fold_in(key, 13), REPLICAS * STEPS * N_INNER)
    return ranks.reshape(REPLICAS, STEPS, BLOCKS).astype(jnp.int32)


def draw_out_count(key, part):
    counts = skewed_counts(jax.random.fold_in(key, 17), (REPLICAS, STEPS))
    fullest = jax.random.randint(jax.random.fold_in(key, 19), (STEPS,), 0, REPLICAS)
    rows = jnp.arange(REPLICAS)[:, None]
    return jnp.where(rows == fullest[None, :], CAP, counts).astype(jnp.int32)


def draw_out_rank(key, part):
    ranks = permutations(jax.random.fold_in(key, 23), REPLICAS * STEPS)
    return ranks.reshape(REPLICAS, STEPS, REGION).astype(jnp.int32)


def block_scale(key, shape, cuts, smallest, largest):
    factor_of, own = 1.0, jax.random.fold_in(key, 6)
    for axis_at, blocks in cuts:
        draws = jnp.exp(jax.random.uniform(jax.random.fold_in(own, axis_at), (blocks,), jnp.float32, smallest / len(cuts), largest / len(cuts)))
        factor_of = factor_of * jnp.repeat(draws, shape[axis_at] // blocks).reshape([-1 if axis == axis_at else 1 for axis in range(len(shape))])
    return factor_of


def normal_values(rng, shape, width, bound, cuts=(), kind=jnp.bfloat16):
    drawn = width * jax.random.normal(rng, shape, jnp.float32)
    if cuts:
        drawn = drawn * block_scale(rng, shape, cuts, -0.22, 0.18)
    return jnp.clip(drawn, -bound, bound).astype(kind)


def setup_inputs(seed: int = 0) -> dict:
    key_of = jax.random.split(jax.random.key(seed), 9)
    return {
        "acts": normal_values(key_of[0], (REPLICAS, STEPS, TOK, TILE_R), 1.0, 6.0, ((0, 512),)),
        "cotangent": normal_values(key_of[1], (REPLICAS, STEPS, TOK, TILE_C), 1.0, 6.0, ((0, 512),)),
        "residual": normal_values(key_of[2], (REPLICAS, BLOCKS, BLOCK), 0.1, 0.6, ((0, 512),), jnp.float32),
        "owner_residual": normal_values(key_of[3], (REPLICAS, REGION, BLOCK), 0.5, 3.0, ((0, 512),), jnp.float32),
        "in_count": draw_in_count(jax.random.fold_in(key_of[8], 71), 0),
        "in_rank": draw_in_rank(jax.random.fold_in(key_of[8], 71), 0),
        "out_count": draw_out_count(jax.random.fold_in(key_of[8], 71), 0),
        "out_rank": draw_out_rank(jax.random.fold_in(key_of[8], 71), 0),
    }


step_size = 0.0625

def local_grad(pair):
    left, right = pair
    return jnp.einsum('tr,tc->rc', left.astype(jnp.float32), right.astype(jnp.float32), precision=lax.Precision.HIGHEST)

def reference(acts, cotangent, residual, owner_residual, in_count, in_rank, out_count, out_rank):
    scale = 1.0 / math.sqrt(TOK * N_INNER)
    resid = residual
    oresid = owner_residual.reshape(N_OUTER, BLOCKS, BLOCK)
    total = jnp.zeros((BLOCKS, BLOCK), jnp.float32)
    for step in range(STEPS):
        grads = lax.map(local_grad, (acts[:, step], cotangent[:, step]))
        accum = resid + (grads * scale).reshape(REPLICAS, BLOCKS, BLOCK)
        counts = jnp.repeat(in_count[:, step], REGION, axis=1)
        chosen = (in_rank[:, step] < counts)[..., None]
        sent = jnp.where(chosen, accum, jnp.float32(0.0))
        resid = jnp.where(chosen, jnp.float32(0.0), accum)
        pod_sum = lax.optimization_barrier(jnp.sum(sent.reshape(N_OUTER, N_INNER, BLOCKS, BLOCK), axis=1))
        owner_acc = pod_sum + oresid
        ocounts = jnp.repeat(out_count[:, step].reshape(N_OUTER, N_INNER), REGION, axis=1)
        passed = (out_rank[:, step].reshape(N_OUTER, BLOCKS) < ocounts)[..., None]
        cross = lax.optimization_barrier(jnp.sum(jnp.where(passed, owner_acc, jnp.float32(0.0)), axis=0))
        oresid = jnp.where(passed, jnp.float32(0.0), owner_acc)
        delta = cross.astype(jnp.bfloat16)
        total = total + delta.astype(jnp.float32)
    applied = (-step_size * total).astype(jnp.bfloat16).reshape(TILE_R, TILE_C)
    return (applied, resid, oresid.reshape(REPLICAS, REGION, BLOCK))
```

```python
import math

import jax
import jax.numpy as jnp
import numpy as np
from jax import lax
from jax.experimental import pallas as pl
from jax.experimental.pallas import tpu as pltpu
from jax.sharding import Mesh
from jax.sharding import PartitionSpec as P

STEP_SIZE = 0.0625
NX, NZ, NY, NC = 4, 8, 8, 2
CHIPS = NZ * NY
REGION = 16
WIDTH = 128
BF = jnp.bfloat16
F32 = jnp.float32
VMEM_LIMIT = 48 * 1024 * 1024


def lines(axes0, axes1):
    ids = np.arange(NX * NZ * NY * NC).reshape(NX, NZ, NY, NC)
    out = []
    for core, axes in ((0, axes0), (1, axes1)):
        sub = ids[..., core]
        size = int(np.prod([sub.shape[a] for a in axes]))
        moved = np.moveaxis(sub, axes, range(3 - len(axes), 3))
        out += moved.reshape(-1, size).tolist()
    return out


def exchange(value, groups):
    return lax.all_to_all(
        value, "d", split_axis=0, concat_axis=0, tiled=True, axis_index_groups=groups
    )


def other_core(value):
    pairs = [(i, i ^ 1) for i in range(NX * NZ * NY * NC)]
    return lax.ppermute(value, "d", pairs)


def place_of(core, z, y):
    return z * NY + y if core == 0 else y * NZ + z


def local_kernel(scale, core_ref, acts_ref, cot_ref, resid_ref, count_ref, rank_ref,
                 resid_out, keep_ref, give_ref, acc_ref, ranks_ref, chosen_ref):
    step = pl.program_id(0)
    core = core_ref[0]
    rows = acts_ref.shape[3]
    cols = cot_ref.shape[3]
    tiles = cols // WIDTH
    groups = resid_ref.shape[1] // WIDTH

    @pl.when(step == 0)
    def _():
        resid_out[...] = resid_ref[...]

    @pl.when(step == 0)
    def _():
        per = WIDTH // groups
        row_id = lax.broadcasted_iota(jnp.int32, (groups, WIDTH), 0)
        lane_id = lax.broadcasted_iota(jnp.int32, (groups, WIDTH), 1)
        owner_id = lax.broadcasted_iota(jnp.int32, (WIDTH, WIDTH), 0) % per
        block_id = lax.broadcasted_iota(jnp.int32, (WIDTH, WIDTH), 1) // REGION
        place = jnp.where(owner_id == block_id, 1.0, 0.0).astype(BF)
        eye = jnp.where(row_id == lane_id, 1.0, 0.0).astype(BF)
        for s in range(chosen_ref.shape[0]):
            for r in range(groups):
                ranks_ref[r:r + 1, :] = rank_ref[0, s:s + 1, r * WIDTH:(r + 1) * WIDTH]
            count = jnp.broadcast_to(count_ref[0, s:s + 1, :].astype(F32), (groups, WIDTH))
            spread = jnp.where(lane_id // per == row_id, count, 0.0)
            limit = jnp.dot(spread.astype(BF), place, preferred_element_type=F32)
            chosen = jnp.where(ranks_ref[...].astype(F32) < limit, 1.0, 0.0)
            chosen_ref[s] = lax.dot_general(chosen.astype(BF), eye, (((0,), (0,)), ((), ())),
                                            preferred_element_type=F32)

    columns = chosen_ref[step]
    left = acts_ref[0, 0]
    half = 2 * WIDTH
    for h in range(cols // half):
        grad = lax.dot_general(left, cot_ref[0, 0, :, h * half:(h + 1) * half],
                               (((0,), (0,)), ((), ())), preferred_element_type=F32)
        grad = grad * scale
        for q in range(2):
            acc_ref[pl.ds(2 * h + q, rows, stride=tiles), :] = grad[:, q * WIDTH:(q + 1) * WIDTH]

    for r in range(groups):
        span = slice(r * WIDTH, (r + 1) * WIDTH)
        total = resid_out[0, span, :] + acc_ref[span, :]
        mask = jnp.broadcast_to(columns[:, r:r + 1], (WIDTH, WIDTH)) > 0.5
        resid_out[0, span, :] = jnp.where(mask, 0.0, total)
        sent = jnp.where(mask, total, 0.0).astype(BF)
        for me in range(NC):
            @pl.when(core == me)
            def _(me=me, r=r, sent=sent):
                for i in range(WIDTH // REGION):
                    owner = r * (WIDTH // REGION) + i
                    z, y, c = owner // (NY * NC), (owner // NC) % NY, owner % NC
                    to = keep_ref if c == me else give_ref
                    to[place_of(c, z, y), step] = sent[i * REGION:(i + 1) * REGION, :]


def owner_kernel(arrived_ref, oresid_ref, count_ref, rank_ref, out_ref, oresid_out):
    steps = rank_ref.shape[1]
    eye = (lax.broadcasted_iota(jnp.int32, (REGION, REGION), 0)
           == lax.broadcasted_iota(jnp.int32, (REGION, REGION), 1))
    oresid = oresid_ref[0]
    for s in range(steps):
        total = arrived_ref[0, s].astype(F32)
        for k in range(1, arrived_ref.shape[0]):
            total = total + arrived_ref[k, s].astype(F32)
        row = jnp.where(rank_ref[0, s:s + 1, :] < count_ref[0, s], 1.0, 0.0)
        square = jnp.where(eye, jnp.broadcast_to(row, (REGION, REGION)), 0.0)
        passed = jnp.broadcast_to(jnp.sum(square, axis=1, keepdims=True), (REGION, WIDTH)) > 0.5
        total = total + oresid
        going = jnp.where(passed, total, 0.0).astype(BF)
        oresid = jnp.where(passed, 0.0, total)
        for k in range(out_ref.shape[0]):
            out_ref[k, s] = going
    oresid_out[0] = oresid


def update_kernel(arrived_ref, out_ref):
    near = out_ref.shape[0]
    for a in range(near):
        total = jnp.zeros((REGION, WIDTH), F32)
        for s in range(arrived_ref.shape[1]):
            cross = arrived_ref[a, s].astype(F32)
            for x in range(1, NX):
                cross = cross + arrived_ref[x * near + a, s].astype(F32)
            total = total + cross.astype(BF).astype(F32)
        applied = (-STEP_SIZE * total).astype(BF)
        for k in range(near):
            out_ref[k, a] = applied


def assemble_kernel(core_ref, own_ref, got_ref, out_ref, flat_ref):
    core = core_ref[0]
    rows, cols = out_ref.shape
    tiles = cols // WIDTH
    for i in range(CHIPS):
        plain = NC * REGION * i
        swapped = NC * REGION * ((i % NZ) * NY + i // NZ) + REGION
        mine = pl.multiple_of(jnp.where(core == 0, plain, swapped), REGION)
        theirs = pl.multiple_of(jnp.where(core == 0, swapped, plain), REGION)
        flat_ref[pl.ds(mine, REGION), :] = own_ref[i].astype(F32)
        flat_ref[pl.ds(theirs, REGION), :] = got_ref[i].astype(F32)
    for t in range(tiles):
        out_ref[:, t * WIDTH:(t + 1) * WIDTH] = flat_ref[pl.ds(t, rows, stride=tiles), :].astype(BF)


def vmem():
    return pl.BlockSpec(memory_space=pltpu.VMEM)


def smem():
    return pl.BlockSpec(memory_space=pltpu.SMEM)


def per_device(acts, cotangent, residual, owner_residual, in_count, in_rank, out_count, out_rank):
    steps, tokens, rows = acts.shape[1:]
    cols = cotangent.shape[3]
    blocks = residual.shape[1]
    scale = 1.0 / math.sqrt(tokens * CHIPS * NC)
    core = (lax.axis_index("d") % NC).astype(jnp.int32).reshape(1)
    params = pltpu.CompilerParams(vmem_limit_bytes=VMEM_LIMIT)

    def local(*args):
        return local_kernel(scale, *args)

    whole3 = lambda s, c: (0, 0, 0)
    whole4 = lambda s, c: (0, 0, 0, 0)
    half = (CHIPS, steps, REGION, WIDTH)
    new_residual, keep, give = pl.pallas_call(
        local,
        grid_spec=pltpu.PrefetchScalarGridSpec(
            num_scalar_prefetch=1,
            grid=(steps,),
            in_specs=[
                pl.BlockSpec((1, 1, tokens, rows), lambda s, c: (0, s, 0, 0)),
                pl.BlockSpec((1, 1, tokens, cols), lambda s, c: (0, s, 0, 0)),
                pl.BlockSpec((1, blocks, WIDTH), whole3),
                pl.BlockSpec(in_count.shape, whole3),
                pl.BlockSpec(in_rank.shape, whole3),
            ],
            out_specs=[
                pl.BlockSpec((1, blocks, WIDTH), whole3),
                pl.BlockSpec(half, whole4),
                pl.BlockSpec(half, whole4),
            ],
            scratch_shapes=[
                pltpu.VMEM((blocks, WIDTH), F32),
                pltpu.VMEM((blocks // WIDTH, WIDTH), jnp.int32),
                pltpu.VMEM((steps, WIDTH, WIDTH), F32),
            ],
        ),
        out_shape=[
            jax.ShapeDtypeStruct(residual.shape, F32),
            jax.ShapeDtypeStruct(half, BF),
            jax.ShapeDtypeStruct(half, BF),
        ],
        compiler_params=params,
        name="local",
    )(core, acts, cotangent, residual, in_count, in_rank)

    got = other_core(give)
    pair = (keep.astype(F32) + got.astype(F32)).astype(BF)
    first = exchange(pair.reshape(NZ, NY, steps, REGION, WIDTH), lines((1,), (2,)))
    line = jnp.sum(first.astype(F32), axis=0).astype(BF)
    second = exchange(line, lines((2,), (1,)))

    outgoing, new_owner = pl.pallas_call(
        owner_kernel,
        in_specs=[vmem(), vmem(), smem(), vmem()],
        out_specs=[vmem(), vmem()],
        out_shape=[
            jax.ShapeDtypeStruct((NX * NY, steps, REGION, WIDTH), BF),
            jax.ShapeDtypeStruct(owner_residual.shape, F32),
        ],
        compiler_params=params,
        name="owner",
    )(second, owner_residual, out_count, out_rank)

    crossing = exchange(outgoing, lines((0, 2), (0, 1)))
    copies = pl.pallas_call(
        update_kernel,
        in_specs=[vmem()],
        out_specs=vmem(),
        out_shape=jax.ShapeDtypeStruct((NZ, NY, REGION, WIDTH), BF),
        compiler_params=params,
        name="update",
    )(crossing)
    own = exchange(copies, lines((1,), (2,))).reshape(CHIPS, REGION, WIDTH)
    theirs = other_core(own)
    applied = pl.pallas_call(
        assemble_kernel,
        in_specs=[smem(), vmem(), vmem()],
        out_specs=vmem(),
        out_shape=jax.ShapeDtypeStruct((rows, cols), BF),
        scratch_shapes=[pltpu.VMEM((blocks, WIDTH), F32)],
        compiler_params=params,
        name="assemble",
    )(core, own, theirs)
    return applied, new_residual, new_owner


def solution(mesh):
    flat = Mesh(mesh.devices.reshape(-1), ("d",))
    spec = P("d")
    return jax.shard_map(
        per_device,
        mesh=flat,
        in_specs=(spec,) * 8,
        out_specs=(P(), spec, spec),
        check_vma=False,
    )
```

```python
import math

import jax
import jax.numpy as jnp
import numpy as np
from jax import lax
from jax.experimental import pallas as pl
from jax.experimental.pallas import tpu as pltpu
from jax.sharding import Mesh
from jax.sharding import PartitionSpec as P

STEP_SIZE = 0.0625
NX, NZ, NY, NC = 4, 8, 8, 2
CHIPS = NZ * NY
REGION = 16
WIDTH = 128
BF = jnp.bfloat16
F32 = jnp.float32
VMEM_LIMIT = 48 * 1024 * 1024


def groups_along(axes):
    ids = np.arange(NX * NZ * NY * NC).reshape(NX, NZ, NY, NC)
    size = int(np.prod([ids.shape[a] for a in axes]))
    return np.moveaxis(ids, axes, range(4 - len(axes), 4)).reshape(-1, size).tolist()


def exchange(value, axes):
    return lax.all_to_all(
        value, "d", split_axis=0, concat_axis=0, tiled=True, axis_index_groups=groups_along(axes)
    )


def other_core(value):
    pairs = [(i, i ^ 1) for i in range(NX * NZ * NY * NC)]
    return lax.ppermute(value, "d", pairs)


def of_both_cores(value):
    return lax.all_gather(value, "d", axis=0, axis_index_groups=groups_along((3,)))


def local_kernel(scale, core_ref, acts_hbm, cot_hbm, resid_hbm, count_hbm, rank_hbm,
                 resid_ref, keep_ref, give_ref,
                 acts_ref, cot_ref, acc_ref, count_ref, rank_ref, ranks_ref, chosen_ref, sems):
    core = core_ref[0]
    steps, _, rows = acts_ref.shape
    cols = cot_ref.shape[2]
    tiles = cols // WIDTH
    groups = resid_ref.shape[1] // WIDTH

    copies = [
        pltpu.make_async_copy(rank_hbm, rank_ref, sems.at[0]),
        pltpu.make_async_copy(count_hbm, count_ref, sems.at[1]),
        pltpu.make_async_copy(resid_hbm, resid_ref, sems.at[2]),
    ]
    for s in range(steps):
        copies.append(pltpu.make_async_copy(acts_hbm.at[0, s], acts_ref.at[s], sems.at[3 + 2 * s]))
        copies.append(pltpu.make_async_copy(cot_hbm.at[0, s], cot_ref.at[s], sems.at[4 + 2 * s]))
    for i in [0, 1, 3, 4, 2] + list(range(5, 3 + 2 * steps)):
        copies[i].start()

    per = WIDTH // groups
    row_id = lax.broadcasted_iota(jnp.int32, (groups, WIDTH), 0)
    lane_id = lax.broadcasted_iota(jnp.int32, (groups, WIDTH), 1)
    owner_id = lax.broadcasted_iota(jnp.int32, (WIDTH, WIDTH), 0) % per
    block_id = lax.broadcasted_iota(jnp.int32, (WIDTH, WIDTH), 1) // REGION
    place = jnp.where(owner_id == block_id, 1.0, 0.0).astype(BF)
    eye = jnp.where(row_id == lane_id, 1.0, 0.0).astype(BF)
    copies[0].wait()
    copies[1].wait()
    for s in range(steps):
        for r in range(groups):
            ranks_ref[s, r:r + 1, :] = rank_ref[0, s:s + 1, r * WIDTH:(r + 1) * WIDTH]
        count = jnp.broadcast_to(count_ref[0, s:s + 1, :].astype(F32), (groups, WIDTH))
        spread = jnp.where(lane_id // per == row_id, count, 0.0)
        limit = jnp.dot(spread.astype(BF), place, preferred_element_type=F32)
        chosen = jnp.where(ranks_ref[s].astype(F32) < limit, 1.0, 0.0)
        chosen_ref[s] = lax.dot_general(chosen.astype(BF), eye, (((0,), (0,)), ((), ())),
                                        preferred_element_type=F32)

    half = 2 * WIDTH
    for s in range(steps):
        copies[3 + 2 * s].wait()
        copies[4 + 2 * s].wait()
        left = acts_ref[s]
        for h in range(cols // half):
            grad = lax.dot_general(left, cot_ref[s, :, h * half:(h + 1) * half],
                                   (((0,), (0,)), ((), ())), preferred_element_type=F32)
            grad = grad * scale
            for q in range(2):
                acc_ref[pl.ds(2 * h + q, rows, stride=tiles), :] = grad[:, q * WIDTH:(q + 1) * WIDTH]
        if s == 0:
            copies[2].wait()
        columns = chosen_ref[s]
        for me in range(NC):
            @pl.when(core == me)
            def _(me=me, s=s, columns=columns):
                for r in range(groups):
                    span = slice(r * WIDTH, (r + 1) * WIDTH)
                    total = resid_ref[0, span, :] + acc_ref[span, :]
                    mask = jnp.broadcast_to(columns[:, r:r + 1], (WIDTH, WIDTH)) > 0.5
                    resid_ref[0, span, :] = jnp.where(mask, 0.0, total)
                    sent = jnp.where(mask, total, 0.0).astype(BF)
                    for i in range(WIDTH // REGION):
                        owner = r * (WIDTH // REGION) + i
                        to = keep_ref if owner % NC == me else give_ref
                        to[owner // NC, s] = sent[i * REGION:(i + 1) * REGION, :]


def owner_kernel(arrived_ref, oresid_ref, count_ref, rank_ref, out_ref, oresid_out):
    steps = rank_ref.shape[1]
    eye = (lax.broadcasted_iota(jnp.int32, (REGION, REGION), 0)
           == lax.broadcasted_iota(jnp.int32, (REGION, REGION), 1))
    oresid = oresid_ref[0]
    for s in range(steps):
        total = arrived_ref[0, s].astype(F32)
        for k in range(1, arrived_ref.shape[0]):
            total = total + arrived_ref[k, s].astype(F32)
        row = jnp.where(rank_ref[0, s:s + 1, :] < count_ref[0, s], 1.0, 0.0)
        square = jnp.where(eye, jnp.broadcast_to(row, (REGION, REGION)), 0.0)
        passed = jnp.broadcast_to(jnp.sum(square, axis=1, keepdims=True), (REGION, WIDTH)) > 0.5
        total = total + oresid
        going = jnp.where(passed, total, 0.0).astype(BF)
        oresid = jnp.where(passed, 0.0, total)
        for k in range(out_ref.shape[0]):
            out_ref[k, s] = going
    oresid_out[0] = oresid


def update_kernel(arrived_ref, out_ref):
    total = jnp.zeros((REGION, WIDTH), F32)
    for s in range(arrived_ref.shape[1]):
        cross = arrived_ref[0, s].astype(F32)
        for x in range(1, NX):
            cross = cross + arrived_ref[x, s].astype(F32)
        total = total + cross.astype(BF).astype(F32)
    applied = (-STEP_SIZE * total).astype(BF)
    for k in range(out_ref.shape[0]):
        out_ref[k] = applied


def assemble_kernel(halves_ref, out_ref, flat_ref):
    rows, cols = out_ref.shape
    tiles = cols // WIDTH
    for i in range(CHIPS):
        for c in range(NC):
            at = (i * NC + c) * REGION
            flat_ref[at:at + REGION, :] = halves_ref[c, i].astype(F32)
    for t in range(tiles):
        out_ref[:, t * WIDTH:(t + 1) * WIDTH] = flat_ref[pl.ds(t, rows, stride=tiles), :].astype(BF)


def vmem():
    return pl.BlockSpec(memory_space=pltpu.VMEM)


def hbm():
    return pl.BlockSpec(memory_space=pltpu.HBM)


def smem():
    return pl.BlockSpec(memory_space=pltpu.SMEM)


def per_device(acts, cotangent, residual, owner_residual, in_count, in_rank, out_count, out_rank):
    steps, tokens, rows = acts.shape[1:]
    cols = cotangent.shape[3]
    blocks = residual.shape[1]
    scale = 1.0 / math.sqrt(tokens * CHIPS * NC)
    core = (lax.axis_index("d") % NC).astype(jnp.int32).reshape(1)
    params = pltpu.CompilerParams(vmem_limit_bytes=VMEM_LIMIT)

    def local(*args):
        return local_kernel(scale, *args)

    half = (CHIPS, steps, REGION, WIDTH)
    new_residual, keep, give = pl.pallas_call(
        local,
        in_specs=[smem(), hbm(), hbm(), hbm(), hbm(), hbm()],
        out_specs=[vmem(), vmem(), vmem()],
        out_shape=[
            jax.ShapeDtypeStruct(residual.shape, F32),
            jax.ShapeDtypeStruct(half, BF),
            jax.ShapeDtypeStruct(half, BF),
        ],
        scratch_shapes=[
            pltpu.VMEM((steps, tokens, rows), BF),
            pltpu.VMEM((steps, tokens, cols), BF),
            pltpu.VMEM((blocks, WIDTH), F32),
            pltpu.VMEM(in_count.shape, jnp.int32),
            pltpu.VMEM(in_rank.shape, jnp.int32),
            pltpu.VMEM((steps, blocks // WIDTH, WIDTH), jnp.int32),
            pltpu.VMEM((steps, WIDTH, WIDTH), F32),
            pltpu.SemaphoreType.DMA((3 + 2 * steps,)),
        ],
        compiler_params=params,
        name="local",
    )(core, *[pltpu.with_memory_space_constraint(v, pltpu.HBM)
            for v in (acts, cotangent, residual, in_count, in_rank)])

    given = other_core(give)
    pair = (keep.astype(F32) + given.astype(F32)).astype(BF)
    arrived = exchange(pair, (1, 2))

    outgoing, new_owner = pl.pallas_call(
        owner_kernel,
        in_specs=[vmem(), vmem(), smem(), vmem()],
        out_specs=[vmem(), vmem()],
        out_shape=[
            jax.ShapeDtypeStruct((NX, steps, REGION, WIDTH), BF),
            jax.ShapeDtypeStruct(owner_residual.shape, F32),
        ],
        compiler_params=params,
        name="owner",
    )(arrived, owner_residual, out_count, out_rank)

    copies = pl.pallas_call(
        update_kernel,
        in_specs=[vmem()],
        out_specs=vmem(),
        out_shape=jax.ShapeDtypeStruct((CHIPS, REGION, WIDTH), BF),
        compiler_params=params,
        name="update",
    )(exchange(outgoing, (0,)))
    halves = of_both_cores(exchange(copies, (1, 2)))
    applied = pl.pallas_call(
        assemble_kernel,
        in_specs=[vmem()],
        out_specs=vmem(),
        out_shape=jax.ShapeDtypeStruct((rows, cols), BF),
        scratch_shapes=[pltpu.VMEM((blocks, WIDTH), F32)],
        compiler_params=params,
        name="assemble",
    )(halves)
    return applied, new_residual, new_owner


def solution(mesh):
    flat = Mesh(mesh.devices.reshape(-1), ("d",))
    spec = P("d")
    return jax.shard_map(
        per_device,
        mesh=flat,
        in_specs=(spec,) * 8,
        out_specs=(P(), spec, spec),
        check_vma=False,
    )
```

```python
import math

import jax
import jax.numpy as jnp
import numpy as np
from jax import lax
from jax.experimental import pallas as pl
from jax.experimental.pallas import tpu as pltpu
from jax.sharding import Mesh
from jax.sharding import PartitionSpec as P

STEP_SIZE = 0.0625
NX, NZ, NY, NC = 4, 8, 8, 2
CHIPS = NZ * NY
REGION = 16
WIDTH = 128
BF = jnp.bfloat16
F32 = jnp.float32
VMEM_LIMIT = 48 * 1024 * 1024


def groups_along(axes):
    ids = np.arange(NX * NZ * NY * NC).reshape(NX, NZ, NY, NC)
    size = int(np.prod([ids.shape[a] for a in axes]))
    return np.moveaxis(ids, axes, range(4 - len(axes), 4)).reshape(-1, size).tolist()


def lines(axes0, axes1):
    return ([g for g in groups_along(axes0) if g[0] % NC == 0]
            + [g for g in groups_along(axes1) if g[0] % NC == 1])


def exchange(value, groups):
    return lax.all_to_all(
        value, "d", split_axis=0, concat_axis=0, tiled=True, axis_index_groups=groups
    )


def from_pod(value, shift):
    ids = np.arange(NX * NZ * NY * NC).reshape(NX, -1)
    pairs = list(zip(ids.reshape(-1).tolist(), np.roll(ids, -shift, axis=0).reshape(-1).tolist()))
    return lax.ppermute(value, "d", pairs)


def place_of(core, z, y):
    return z * NY + y if core == 0 else y * NZ + z


def other_core(value):
    pairs = [(i, i ^ 1) for i in range(NX * NZ * NY * NC)]
    return lax.ppermute(value, "d", pairs)


def of_both_cores(value):
    return lax.all_gather(value, "d", axis=0, axis_index_groups=groups_along((3,)))


def local_kernel(scale, core_ref, acts_hbm, cot_hbm, resid_hbm, count_hbm, rank_hbm,
                 resid_ref, keep_ref, give_ref,
                 acts_ref, cot_ref, acc_ref, count_ref, rank_ref, ranks_ref, chosen_ref, sems):
    core = core_ref[0]
    steps, _, rows = acts_ref.shape
    cols = cot_ref.shape[2]
    tiles = cols // WIDTH
    groups = resid_ref.shape[1] // WIDTH

    copies = [
        pltpu.make_async_copy(rank_hbm, rank_ref, sems.at[0]),
        pltpu.make_async_copy(count_hbm, count_ref, sems.at[1]),
        pltpu.make_async_copy(resid_hbm, resid_ref, sems.at[2]),
    ]
    for s in range(steps):
        copies.append(pltpu.make_async_copy(acts_hbm.at[0, s], acts_ref.at[s], sems.at[3 + 2 * s]))
        copies.append(pltpu.make_async_copy(cot_hbm.at[0, s], cot_ref.at[s], sems.at[4 + 2 * s]))
    for i in [0, 1, 3, 4, 2] + list(range(5, 3 + 2 * steps)):
        copies[i].start()

    per = WIDTH // groups
    row_id = lax.broadcasted_iota(jnp.int32, (groups, WIDTH), 0)
    lane_id = lax.broadcasted_iota(jnp.int32, (groups, WIDTH), 1)
    owner_id = lax.broadcasted_iota(jnp.int32, (WIDTH, WIDTH), 0) % per
    block_id = lax.broadcasted_iota(jnp.int32, (WIDTH, WIDTH), 1) // REGION
    place = jnp.where(owner_id == block_id, 1.0, 0.0).astype(BF)
    eye = jnp.where(row_id == lane_id, 1.0, 0.0).astype(BF)
    copies[0].wait()
    copies[1].wait()
    for s in range(steps):
        for r in range(groups):
            ranks_ref[s, r:r + 1, :] = rank_ref[0, s:s + 1, r * WIDTH:(r + 1) * WIDTH]
        count = jnp.broadcast_to(count_ref[0, s:s + 1, :].astype(F32), (groups, WIDTH))
        spread = jnp.where(lane_id // per == row_id, count, 0.0)
        limit = jnp.dot(spread.astype(BF), place, preferred_element_type=F32)
        chosen = jnp.where(ranks_ref[s].astype(F32) < limit, 1.0, 0.0)
        chosen_ref[s] = lax.dot_general(chosen.astype(BF), eye, (((0,), (0,)), ((), ())),
                                        preferred_element_type=F32)

    half = 2 * WIDTH
    for s in range(steps):
        copies[3 + 2 * s].wait()
        copies[4 + 2 * s].wait()
        left = acts_ref[s]
        for h in range(cols // half):
            grad = lax.dot_general(left, cot_ref[s, :, h * half:(h + 1) * half],
                                   (((0,), (0,)), ((), ())), preferred_element_type=F32)
            grad = grad * scale
            for q in range(2):
                acc_ref[pl.ds(2 * h + q, rows, stride=tiles), :] = grad[:, q * WIDTH:(q + 1) * WIDTH]
        if s == 0:
            copies[2].wait()
        columns = chosen_ref[s]
        for me in range(NC):
            @pl.when(core == me)
            def _(me=me, s=s, columns=columns):
                for r in range(groups):
                    span = slice(r * WIDTH, (r + 1) * WIDTH)
                    total = resid_ref[0, span, :] + acc_ref[span, :]
                    mask = jnp.broadcast_to(columns[:, r:r + 1], (WIDTH, WIDTH)) > 0.5
                    resid_ref[0, span, :] = jnp.where(mask, 0.0, total)
                    sent = jnp.where(mask, total, 0.0).astype(BF)
                    for i in range(WIDTH // REGION):
                        owner = r * (WIDTH // REGION) + i
                        z, y, c = owner // (NY * NC), (owner // NC) % NY, owner % NC
                        at = (place_of(c, z, y) * steps + s) * REGION
                        to = keep_ref if c == me else give_ref
                        to[at:at + REGION, :] = sent[i * REGION:(i + 1) * REGION, :]


def store_kernel(after_ref, value_ref, out_hbm, sem):
    copy = pltpu.make_async_copy(value_ref, out_hbm, sem)
    copy.start()
    copy.wait()


def facts_kernel(after_ref, oresid_ref, count_ref, rank_ref, out_ref):
    eye = (lax.broadcasted_iota(jnp.int32, (REGION, REGION), 0)
           == lax.broadcasted_iota(jnp.int32, (REGION, REGION), 1))
    code = jnp.zeros((REGION, 1), F32)
    for s in range(rank_ref.shape[1]):
        count = jnp.broadcast_to(count_ref[0:1, s:s + 1], (1, REGION))
        row = jnp.where(rank_ref[0, s:s + 1, :] < count, float(1 << s), 0.0)
        square = jnp.where(eye, jnp.broadcast_to(row, (REGION, REGION)), 0.0)
        code = code + jnp.sum(square, axis=1, keepdims=True)
    out_ref[0] = oresid_ref[0]
    out_ref[1] = jnp.broadcast_to(code, (REGION, WIDTH))


def line_kernel(arrived_ref, out_ref):
    peers, near, steps = arrived_ref.shape[:3]
    for a in range(near):
        for s in range(steps):
            total = arrived_ref[0, a, s].astype(F32)
            for k in range(1, peers):
                total = total + arrived_ref[k, a, s].astype(F32)
            part = total.astype(BF)
            for x in range(NX):
                out_ref[x * near + a, s] = part


def owner_kernel(pod_ref, arrived_ref, *refs):
    facts, (copies_ref, last_ref, keeps_ref, all_ref, lasts_ref) = refs[:NX], refs[NX:]
    pod = pod_ref[0]
    for k in range(NX):
        all_ref[(pod + (NX - k)) % NX] = facts[k][...]
    near = arrived_ref.shape[0] // NX
    crosses = [jnp.zeros((REGION, WIDTH), F32) for _ in range(2)]
    for x in range(NX):
        oresid = all_ref[x, 0]
        code = all_ref[x, 1]
        passes = [(code == 1.0) | (code == 3.0), code >= 2.0]
        for s in range(2):
            total = arrived_ref[x * near, s].astype(F32)
            for k in range(1, near):
                total = total + arrived_ref[x * near + k, s].astype(F32)
            total = total + oresid
            crosses[s] = crosses[s] + jnp.where(passes[s], total, 0.0)
            oresid = jnp.where(passes[s], 0.0, total)
            if s == 1:
                lasts_ref[x] = total
    total = crosses[0].astype(BF).astype(F32) + crosses[1].astype(BF).astype(F32)
    applied = (-STEP_SIZE * total).astype(BF)
    for k in range(copies_ref.shape[0]):
        copies_ref[k] = applied
    last_ref[...] = lasts_ref[pod]
    keeps_ref[...] = jnp.where(all_ref[pod, 1] >= 2.0, 0.0, 1.0)


def assemble_kernel(halves_ref, out_ref, flat_ref):
    rows, cols = out_ref.shape
    tiles = cols // WIDTH
    for i in range(CHIPS):
        for c in range(NC):
            at = (i * NC + c) * REGION
            flat_ref[at:at + REGION, :] = halves_ref[c, i].astype(F32)
    for t in range(tiles):
        out_ref[:, t * WIDTH:(t + 1) * WIDTH] = flat_ref[pl.ds(t, rows, stride=tiles), :].astype(BF)


def vmem():
    return pl.BlockSpec(memory_space=pltpu.VMEM)


def anywhere():
    return pl.BlockSpec(memory_space=pl.ANY)


def hbm():
    return pl.BlockSpec(memory_space=pltpu.HBM)


def smem():
    return pl.BlockSpec(memory_space=pltpu.SMEM)


def per_device(acts, cotangent, residual, owner_residual, in_count, in_rank, out_count, out_rank):
    steps, tokens, rows = acts.shape[1:]
    cols = cotangent.shape[3]
    blocks = residual.shape[1]
    scale = 1.0 / math.sqrt(tokens * CHIPS * NC)
    core = (lax.axis_index("d") % NC).astype(jnp.int32).reshape(1)
    params = pltpu.CompilerParams(vmem_limit_bytes=VMEM_LIMIT)

    def local(*args):
        return local_kernel(scale, *args)

    pod = (lax.axis_index("d") // (CHIPS * NC)).astype(jnp.int32).reshape(1)
    size = CHIPS * steps * REGION
    new_resid, keep, give = pl.pallas_call(
        local,
        in_specs=[smem(), hbm(), hbm(), hbm(), hbm(), hbm()],
        out_specs=[vmem(), vmem(), vmem()],
        out_shape=[
            jax.ShapeDtypeStruct(residual.shape, F32),
            jax.ShapeDtypeStruct((size, WIDTH), BF),
            jax.ShapeDtypeStruct((size, WIDTH), BF),
        ],
        scratch_shapes=[
            pltpu.VMEM((steps, tokens, rows), BF),
            pltpu.VMEM((steps, tokens, cols), BF),
            pltpu.VMEM((blocks, WIDTH), F32),
            pltpu.VMEM(in_count.shape, jnp.int32),
            pltpu.VMEM(in_rank.shape, jnp.int32),
            pltpu.VMEM((steps, blocks // WIDTH, WIDTH), jnp.int32),
            pltpu.VMEM((steps, WIDTH, WIDTH), F32),
            pltpu.SemaphoreType.DMA((3 + 2 * steps,)),
        ],
        compiler_params=params,
        name="local",
    )(core, *[pltpu.with_memory_space_constraint(v, pltpu.HBM)
              for v in (acts, cotangent, residual, in_count, in_rank)])

    given = other_core(give)
    pair = (keep.astype(F32) + given.astype(F32)).astype(BF)
    first = exchange(pair.reshape(NZ, NY, steps, REGION, WIDTH), lines((1,), (2,)))

    facts = pl.pallas_call(
        facts_kernel,
        in_specs=[anywhere(), vmem(), vmem(), vmem()],
        out_specs=vmem(),
        out_shape=jax.ShapeDtypeStruct((2, REGION, WIDTH), F32),
        compiler_params=params,
        name="facts",
    )(pair, owner_residual, out_count, out_rank)
    facts = [facts] + [from_pod(facts, k) for k in range(1, NX)]

    line = pl.pallas_call(
        line_kernel,
        in_specs=[vmem()],
        out_specs=vmem(),
        out_shape=jax.ShapeDtypeStruct((NX * NY, steps, REGION, WIDTH), BF),
        compiler_params=params,
        name="line",
    )(first)
    second = exchange(line, lines((0, 2), (0, 1)))
    new_residual = pl.pallas_call(
        store_kernel,
        in_specs=[anywhere(), vmem()],
        out_specs=hbm(),
        out_shape=jax.ShapeDtypeStruct(residual.shape, F32),
        scratch_shapes=[pltpu.SemaphoreType.DMA],
        compiler_params=params,
        name="store",
    )(line, new_resid)

    tile = jax.ShapeDtypeStruct((REGION, WIDTH), F32)
    copies, last, keeps = pl.pallas_call(
        owner_kernel,
        in_specs=[smem()] + [vmem()] * (1 + NX),
        out_specs=[vmem(), vmem(), vmem()],
        out_shape=[jax.ShapeDtypeStruct((CHIPS, REGION, WIDTH), BF), tile, tile],
        scratch_shapes=[
            pltpu.VMEM((NX, 2, REGION, WIDTH), F32),
            pltpu.VMEM((NX, REGION, WIDTH), F32),
        ],
        compiler_params=params,
        name="owner",
    )(pod, second, *facts)
    new_owner = jnp.where(keeps > 0.5, last, 0.0)[None]

    halves = of_both_cores(exchange(copies, groups_along((1, 2))))
    applied = pl.pallas_call(
        assemble_kernel,
        in_specs=[vmem()],
        out_specs=vmem(),
        out_shape=jax.ShapeDtypeStruct((rows, cols), BF),
        scratch_shapes=[pltpu.VMEM((blocks, WIDTH), F32)],
        compiler_params=params,
        name="assemble",
    )(halves)
    return applied, new_residual, new_owner


def solution(mesh):
    flat = Mesh(mesh.devices.reshape(-1), ("d",))
    spec = P("d")
    return jax.shard_map(
        per_device,
        mesh=flat,
        in_specs=(spec,) * 8,
        out_specs=(P(), spec, spec),
        check_vma=False,
    )
```

```python
import math

import jax
import jax.numpy as jnp
import numpy as np
from jax import lax
from jax.experimental import pallas as pl
from jax.experimental.pallas import tpu as pltpu
from jax.sharding import Mesh
from jax.sharding import PartitionSpec as P

STEP_SIZE = 0.0625
NX, NZ, NY, NC = 4, 8, 8, 2
CHIPS = NZ * NY
REGION = 16
WIDTH = 128
BF = jnp.bfloat16
F32 = jnp.float32
VMEM_LIMIT = 48 * 1024 * 1024


def groups_along(axes):
    ids = np.arange(NX * NZ * NY * NC).reshape(NX, NZ, NY, NC)
    size = int(np.prod([ids.shape[a] for a in axes]))
    return np.moveaxis(ids, axes, range(4 - len(axes), 4)).reshape(-1, size).tolist()


def exchange(value, axes):
    return lax.all_to_all(
        value, "d", split_axis=0, concat_axis=0, tiled=True, axis_index_groups=groups_along(axes)
    )


def other_core(value):
    pairs = [(i, i ^ 1) for i in range(NX * NZ * NY * NC)]
    return lax.ppermute(value, "d", pairs)


def of_both_cores(value):
    return lax.all_gather(value, "d", axis=0, axis_index_groups=groups_along((3,)))


def local_kernel(scale, core_ref, acts_hbm, cot_hbm, resid_hbm, count_hbm, rank_hbm,
                 resid_ref, keep_ref, give_ref,
                 acts_ref, cot_ref, acc_ref, count_ref, rank_ref, ranks_ref, chosen_ref, sems):
    core = core_ref[0]
    steps, _, rows = acts_ref.shape
    cols = cot_ref.shape[2]
    tiles = cols // WIDTH
    groups = resid_ref.shape[1] // WIDTH
    parts = 2
    part = rows // parts

    def copy(source, target, at):
        return pltpu.make_async_copy(source, target, sems.at[at])

    rank_copy = copy(rank_hbm, rank_ref, 0)
    count_copy = copy(count_hbm, count_ref, 1)
    resid_copy = copy(resid_hbm, resid_ref, 2)
    cot_copy, acts_copy = [], []
    for s in range(steps):
        base = 3 + s * (1 + parts)
        cot_copy.append(copy(cot_hbm.at[0, s], cot_ref.at[s], base))
        acts_copy.append([
            copy(acts_hbm.at[0, s, :, m * part:(m + 1) * part],
                 acts_ref.at[s, :, m * part:(m + 1) * part], base + 1 + m)
            for m in range(parts)
        ])
    rank_copy.start()
    count_copy.start()
    for s in range(steps):
        cot_copy[s].start()
        for m in range(parts):
            acts_copy[s][m].start()
        if s == 0:
            resid_copy.start()

    per = WIDTH // groups
    row_id = lax.broadcasted_iota(jnp.int32, (groups, WIDTH), 0)
    lane_id = lax.broadcasted_iota(jnp.int32, (groups, WIDTH), 1)
    owner_id = lax.broadcasted_iota(jnp.int32, (WIDTH, WIDTH), 0) % per
    block_id = lax.broadcasted_iota(jnp.int32, (WIDTH, WIDTH), 1) // REGION
    place = jnp.where(owner_id == block_id, 1.0, 0.0).astype(BF)
    eye = jnp.where(row_id == lane_id, 1.0, 0.0).astype(BF)
    rank_copy.wait()
    count_copy.wait()
    for s in range(steps):
        for r in range(groups):
            ranks_ref[s, r:r + 1, :] = rank_ref[0, s:s + 1, r * WIDTH:(r + 1) * WIDTH]
        count = jnp.broadcast_to(count_ref[0, s:s + 1, :].astype(F32), (groups, WIDTH))
        spread = jnp.where(lane_id // per == row_id, count, 0.0)
        limit = jnp.dot(spread.astype(BF), place, preferred_element_type=F32)
        chosen = jnp.where(ranks_ref[s].astype(F32) < limit, 1.0, 0.0)
        chosen_ref[s] = lax.dot_general(chosen.astype(BF), eye, (((0,), (0,)), ((), ())),
                                        preferred_element_type=F32)

    half = 2 * WIDTH
    for s in range(steps):
        cot_copy[s].wait()
        for m in range(parts):
            acts_copy[s][m].wait()
            left = acts_ref[s, :, m * part:(m + 1) * part]
            for h in range(cols // half):
                grad = lax.dot_general(left, cot_ref[s, :, h * half:(h + 1) * half],
                                       (((0,), (0,)), ((), ())), preferred_element_type=F32)
                grad = grad * scale
                for q in range(2):
                    to = pl.ds(m * part * tiles + 2 * h + q, part, stride=tiles)
                    acc_ref[to, :] = grad[:, q * WIDTH:(q + 1) * WIDTH]
            if s == 0 and m == 0:
                resid_copy.wait()
            columns = chosen_ref[s]
            for me in range(NC):
                @pl.when(core == me)
                def _(me=me, s=s, m=m, columns=columns):
                    for r in range(m * groups // parts, (m + 1) * groups // parts):
                        span = slice(r * WIDTH, (r + 1) * WIDTH)
                        total = resid_ref[0, span, :] + acc_ref[span, :]
                        mask = jnp.broadcast_to(columns[:, r:r + 1], (WIDTH, WIDTH)) > 0.5
                        resid_ref[0, span, :] = jnp.where(mask, 0.0, total)
                        sent = jnp.where(mask, total, 0.0).astype(BF)
                        for i in range(WIDTH // REGION):
                            owner = r * (WIDTH // REGION) + i
                            to = keep_ref if owner % NC == me else give_ref
                            to[owner // NC, s] = sent[i * REGION:(i + 1) * REGION, :]


def store_kernel(value_ref, out_hbm, sem):
    copy = pltpu.make_async_copy(value_ref, out_hbm, sem)
    copy.start()
    copy.wait()


def owner_kernel(arrived_ref, oresid_ref, count_ref, rank_ref, out_ref, last_ref, kept_ref):
    eye = (lax.broadcasted_iota(jnp.int32, (REGION, REGION), 0)
           == lax.broadcasted_iota(jnp.int32, (REGION, REGION), 1))
    oresid = oresid_ref[0]
    for s in range(rank_ref.shape[1]):
        total = arrived_ref[0, s].astype(F32)
        for k in range(1, arrived_ref.shape[0]):
            total = total + arrived_ref[k, s].astype(F32)
        count = jnp.broadcast_to(count_ref[0:1, s:s + 1], (1, REGION))
        row = jnp.where(rank_ref[0, s:s + 1, :] < count, 1.0, 0.0)
        square = jnp.where(eye, jnp.broadcast_to(row, (REGION, REGION)), 0.0)
        passed = jnp.broadcast_to(jnp.sum(square, axis=1, keepdims=True), (REGION, WIDTH)) > 0.5
        total = total + oresid
        going = jnp.where(passed, total, 0.0).astype(BF)
        oresid = jnp.where(passed, 0.0, total)
        for k in range(out_ref.shape[0]):
            out_ref[k, s] = going
    last_ref[...] = total
    kept_ref[...] = jnp.where(passed, 0.0, 1.0)


def update_kernel(arrived_ref, out_ref):
    total = jnp.zeros((REGION, WIDTH), F32)
    for s in range(arrived_ref.shape[1]):
        cross = arrived_ref[0, s].astype(F32)
        for x in range(1, NX):
            cross = cross + arrived_ref[x, s].astype(F32)
        total = total + cross.astype(BF).astype(F32)
    applied = (-STEP_SIZE * total).astype(BF)
    for k in range(out_ref.shape[0]):
        out_ref[k] = applied


def assemble_kernel(halves_ref, last_ref, kept_ref, out_hbm, oresid_ref, flat_ref, rows_ref, sems):
    oresid_ref[0] = jnp.where(kept_ref[...] > 0.5, last_ref[...], 0.0)
    rows, cols = rows_ref.shape
    tiles = cols // WIDTH
    parts = sems.shape[0]
    part = rows // parts
    sends = []
    for p in range(parts):
        for i in range(p * CHIPS // parts, (p + 1) * CHIPS // parts):
            for c in range(NC):
                at = (i * NC + c) * REGION
                flat_ref[at:at + REGION, :] = halves_ref[c, i].astype(F32)
        span = slice(p * part, (p + 1) * part)
        for t in range(tiles):
            value = flat_ref[pl.ds(p * part * tiles + t, part, stride=tiles), :]
            rows_ref[span, t * WIDTH:(t + 1) * WIDTH] = value.astype(BF)
        sends.append(pltpu.make_async_copy(rows_ref.at[span], out_hbm.at[span], sems.at[p]))
        sends[-1].start()
    for send in sends:
        send.wait()


def vmem():
    return pl.BlockSpec(memory_space=pltpu.VMEM)


def hbm():
    return pl.BlockSpec(memory_space=pltpu.HBM)


def smem():
    return pl.BlockSpec(memory_space=pltpu.SMEM)


def per_device(acts, cotangent, residual, owner_residual, in_count, in_rank, out_count, out_rank):
    steps, tokens, rows = acts.shape[1:]
    cols = cotangent.shape[3]
    blocks = residual.shape[1]
    scale = 1.0 / math.sqrt(tokens * CHIPS * NC)
    core = (lax.axis_index("d") % NC).astype(jnp.int32).reshape(1)
    params = pltpu.CompilerParams(vmem_limit_bytes=VMEM_LIMIT)

    def local(*args):
        return local_kernel(scale, *args)

    half = (CHIPS, steps, REGION, WIDTH)
    new_resid, keep, give = pl.pallas_call(
        local,
        in_specs=[smem(), hbm(), hbm(), hbm(), hbm(), hbm()],
        out_specs=[vmem(), vmem(), vmem()],
        out_shape=[
            jax.ShapeDtypeStruct(residual.shape, F32),
            jax.ShapeDtypeStruct(half, BF),
            jax.ShapeDtypeStruct(half, BF),
        ],
        scratch_shapes=[
            pltpu.VMEM((steps, tokens, rows), BF),
            pltpu.VMEM((steps, tokens, cols), BF),
            pltpu.VMEM((blocks, WIDTH), F32),
            pltpu.VMEM(in_count.shape, jnp.int32),
            pltpu.VMEM(in_rank.shape, jnp.int32),
            pltpu.VMEM((steps, blocks // WIDTH, WIDTH), jnp.int32),
            pltpu.VMEM((steps, WIDTH, WIDTH), F32),
            pltpu.SemaphoreType.DMA((3 + 3 * steps,)),
        ],
        compiler_params=params,
        name="local",
    )(core, *[pltpu.with_memory_space_constraint(v, pltpu.HBM)
            for v in (acts, cotangent, residual, in_count, in_rank)])

    given = other_core(give)
    new_residual = pl.pallas_call(
        store_kernel,
        in_specs=[vmem()],
        out_specs=hbm(),
        out_shape=jax.ShapeDtypeStruct(residual.shape, F32),
        scratch_shapes=[pltpu.SemaphoreType.DMA],
        compiler_params=params,
        name="store",
    )(new_resid)
    pair = (keep.astype(F32) + given.astype(F32)).astype(BF)
    pair, new_residual = lax.optimization_barrier((pair, new_residual))
    arrived = exchange(pair, (1, 2))

    tile = jax.ShapeDtypeStruct((REGION, WIDTH), F32)
    outgoing, last, kept = pl.pallas_call(
        owner_kernel,
        in_specs=[vmem(), vmem(), vmem(), vmem()],
        out_specs=[vmem(), vmem(), vmem()],
        out_shape=[jax.ShapeDtypeStruct((NX, steps, REGION, WIDTH), BF), tile, tile],
        compiler_params=params,
        name="owner",
    )(arrived, owner_residual, out_count, out_rank)

    copies = pl.pallas_call(
        update_kernel,
        in_specs=[vmem()],
        out_specs=vmem(),
        out_shape=jax.ShapeDtypeStruct((CHIPS, REGION, WIDTH), BF),
        compiler_params=params,
        name="update",
    )(exchange(outgoing, (0,)))
    halves = of_both_cores(exchange(copies, (1, 2)))
    applied, new_owner = pl.pallas_call(
        assemble_kernel,
        in_specs=[vmem(), vmem(), vmem()],
        out_specs=[hbm(), vmem()],
        out_shape=[
            jax.ShapeDtypeStruct((rows, cols), BF),
            jax.ShapeDtypeStruct(owner_residual.shape, F32),
        ],
        scratch_shapes=[
            pltpu.VMEM((blocks, WIDTH), F32),
            pltpu.VMEM((rows, cols), BF),
            pltpu.SemaphoreType.DMA((4,)),
        ],
        compiler_params=params,
        name="assemble",
    )(halves, last, kept)
    return applied, new_residual, new_owner


def solution(mesh):
    flat = Mesh(mesh.devices.reshape(-1), ("d",))
    spec = P("d")
    return jax.shard_map(
        per_device,
        mesh=flat,
        in_specs=(spec,) * 8,
        out_specs=(P(), spec, spec),
        check_vma=False,
    )
```

```python
import math

import jax
import jax.numpy as jnp
import numpy as np
from jax import lax
from jax.experimental import pallas as pl
from jax.experimental.pallas import tpu as pltpu
from jax.sharding import Mesh
from jax.sharding import PartitionSpec as P

STEP_SIZE = 0.0625
NX, NZ, NY, NC = 4, 8, 8, 2
CHIPS = NZ * NY
REGION = 16
WIDTH = 128
BF = jnp.bfloat16
F32 = jnp.float32
PART = 512
VMEM_LIMIT = 48 * 1024 * 1024


def groups_along(axes):
    ids = np.arange(NX * NZ * NY * NC).reshape(NX, NZ, NY, NC)
    size = int(np.prod([ids.shape[a] for a in axes]))
    return np.moveaxis(ids, axes, range(4 - len(axes), 4)).reshape(-1, size).tolist()


def lines(axes0, axes1):
    return ([g for g in groups_along(axes0) if g[0] % NC == 0]
            + [g for g in groups_along(axes1) if g[0] % NC == 1])


def exchange(value, groups):
    return lax.all_to_all(
        value, "d", split_axis=0, concat_axis=0, tiled=True, axis_index_groups=groups
    )


def place_of(core, z, y):
    return z * NY + y if core == 0 else y * NZ + z


def other_core(value):
    pairs = [(i, i ^ 1) for i in range(NX * NZ * NY * NC)]
    return lax.ppermute(value, "d", pairs)


def of_both_cores(value):
    return lax.all_gather(value, "d", axis=0, axis_index_groups=groups_along((3,)))


def local_kernel(scale, core_ref, acts_hbm, cot_hbm, resid_hbm, count_hbm, rank_hbm,
                 resid_ref, keep_ref, give_ref,
                 acts_ref, cot_ref, acc_ref, count_ref, rank_ref, ranks_ref, chosen_ref, sems):
    core = core_ref[0]
    steps, _, rows = acts_ref.shape
    cols = cot_ref.shape[2]
    tiles = cols // WIDTH
    groups = resid_ref.shape[1] // WIDTH
    parts = resid_ref.shape[1] // PART

    def copy(source, target, at):
        return pltpu.make_async_copy(source, target, sems.at[at])

    rank_copy = copy(rank_hbm, rank_ref, 0)
    count_copy = copy(count_hbm, count_ref, 1)
    acts_copy = [copy(acts_hbm.at[0, s], acts_ref.at[s], 2 + 2 * s) for s in range(steps)]
    cot_copy = [copy(cot_hbm.at[0, s], cot_ref.at[s], 3 + 2 * s) for s in range(steps)]
    resid_copy = [
        copy(resid_hbm.at[:, p * PART:(p + 1) * PART], resid_ref.at[:, p * PART:(p + 1) * PART],
             2 + 2 * steps + p)
        for p in range(parts)
    ]
    rank_copy.start()
    count_copy.start()
    for s in range(steps):
        acts_copy[s].start()
        cot_copy[s].start()
    for p in range(parts):
        resid_copy[p].start()

    per = WIDTH // groups
    row_id = lax.broadcasted_iota(jnp.int32, (groups, WIDTH), 0)
    lane_id = lax.broadcasted_iota(jnp.int32, (groups, WIDTH), 1)
    owner_id = lax.broadcasted_iota(jnp.int32, (WIDTH, WIDTH), 0) % per
    block_id = lax.broadcasted_iota(jnp.int32, (WIDTH, WIDTH), 1) // REGION
    place = jnp.where(owner_id == block_id, 1.0, 0.0).astype(BF)
    eye = jnp.where(row_id == lane_id, 1.0, 0.0).astype(BF)
    rank_copy.wait()
    count_copy.wait()
    for s in range(steps):
        for r in range(groups):
            ranks_ref[s, r:r + 1, :] = rank_ref[0, s:s + 1, r * WIDTH:(r + 1) * WIDTH]
        count = jnp.broadcast_to(count_ref[0, s:s + 1, :].astype(F32), (groups, WIDTH))
        spread = jnp.where(lane_id // per == row_id, count, 0.0)
        limit = jnp.dot(spread.astype(BF), place, preferred_element_type=F32)
        chosen = jnp.where(ranks_ref[s].astype(F32) < limit, 1.0, 0.0)
        chosen_ref[s] = lax.dot_general(chosen.astype(BF), eye, (((0,), (0,)), ((), ())),
                                        preferred_element_type=F32)

    half = 2 * WIDTH
    for s in range(steps):
        acts_copy[s].wait()
        cot_copy[s].wait()
        left = acts_ref[s]
        for h in range(cols // half):
            grad = lax.dot_general(left, cot_ref[s, :, h * half:(h + 1) * half],
                                   (((0,), (0,)), ((), ())), preferred_element_type=F32)
            grad = grad * scale
            for q in range(2):
                to = pl.ds(2 * h + q, rows, stride=tiles)
                acc_ref[s, to, :] = grad[:, q * WIDTH:(q + 1) * WIDTH]

    columns = [chosen_ref[s] for s in range(steps)]
    for p in range(parts):
        resid_copy[p].wait()
        for me in range(NC):
            @pl.when(core == me)
            def _(me=me, p=p):
                for r in range(p * groups // parts, (p + 1) * groups // parts):
                    span = slice(r * WIDTH, (r + 1) * WIDTH)
                    total = resid_ref[0, span, :]
                    for s in range(steps):
                        total = total + acc_ref[s, span, :]
                        mask = jnp.broadcast_to(columns[s][:, r:r + 1], (WIDTH, WIDTH)) > 0.5
                        sent = jnp.where(mask, total, 0.0).astype(BF)
                        total = jnp.where(mask, 0.0, total)
                        for i in range(WIDTH // REGION):
                            owner = r * (WIDTH // REGION) + i
                            z, y, c = owner // (NY * NC), (owner // NC) % NY, owner % NC
                            to = keep_ref if c == me else give_ref
                            to[place_of(c, z, y), s] = sent[i * REGION:(i + 1) * REGION, :]
                    resid_ref[0, span, :] = total


def store_kernel(value_ref, out_hbm, sem):
    copy = pltpu.make_async_copy(value_ref, out_hbm, sem)
    copy.start()
    copy.wait()


def owner_kernel(arrived_ref, oresid_ref, count_ref, rank_ref, out_ref, last_ref, kept_ref):
    eye = (lax.broadcasted_iota(jnp.int32, (REGION, REGION), 0)
           == lax.broadcasted_iota(jnp.int32, (REGION, REGION), 1))
    oresid = oresid_ref[0]
    for s in range(rank_ref.shape[1]):
        total = arrived_ref[0, s].astype(F32)
        for k in range(1, arrived_ref.shape[0]):
            total = total + arrived_ref[k, s].astype(F32)
        count = jnp.broadcast_to(count_ref[0:1, s:s + 1], (1, REGION))
        row = jnp.where(rank_ref[0, s:s + 1, :] < count, 1.0, 0.0)
        square = jnp.where(eye, jnp.broadcast_to(row, (REGION, REGION)), 0.0)
        passed = jnp.broadcast_to(jnp.sum(square, axis=1, keepdims=True), (REGION, WIDTH)) > 0.5
        total = total + oresid
        going = jnp.where(passed, total, 0.0).astype(BF)
        oresid = jnp.where(passed, 0.0, total)
        for k in range(out_ref.shape[0]):
            out_ref[k, s] = going
    last_ref[...] = total
    kept_ref[...] = jnp.where(passed, 0.0, 1.0)


def update_kernel(arrived_ref, out_ref):
    total = jnp.zeros((REGION, WIDTH), F32)
    for s in range(arrived_ref.shape[1]):
        cross = arrived_ref[0, s].astype(F32)
        for x in range(1, NX):
            cross = cross + arrived_ref[x, s].astype(F32)
        total = total + cross.astype(BF).astype(F32)
    applied = (-STEP_SIZE * total).astype(BF)
    for k in range(out_ref.shape[0]):
        out_ref[k] = applied


def assemble_kernel(halves_ref, last_ref, kept_ref, out_ref, oresid_ref, flat_ref):
    oresid_ref[0] = jnp.where(kept_ref[...] > 0.5, last_ref[...], 0.0)
    rows, cols = out_ref.shape
    tiles = cols // WIDTH
    for i in range(CHIPS):
        for c in range(NC):
            at = (i * NC + c) * REGION
            flat_ref[at:at + REGION, :] = halves_ref[c, i].astype(F32)
    for t in range(tiles):
        out_ref[:, t * WIDTH:(t + 1) * WIDTH] = flat_ref[pl.ds(t, rows, stride=tiles), :].astype(BF)


def vmem():
    return pl.BlockSpec(memory_space=pltpu.VMEM)


def hbm():
    return pl.BlockSpec(memory_space=pltpu.HBM)


def smem():
    return pl.BlockSpec(memory_space=pltpu.SMEM)


def per_device(acts, cotangent, residual, owner_residual, in_count, in_rank, out_count, out_rank):
    steps, tokens, rows = acts.shape[1:]
    cols = cotangent.shape[3]
    blocks = residual.shape[1]
    scale = 1.0 / math.sqrt(tokens * CHIPS * NC)
    core = (lax.axis_index("d") % NC).astype(jnp.int32).reshape(1)
    params = pltpu.CompilerParams(vmem_limit_bytes=VMEM_LIMIT)

    def local(*args):
        return local_kernel(scale, *args)

    half = (CHIPS, steps, REGION, WIDTH)
    new_resid, keep, give = pl.pallas_call(
        local,
        in_specs=[smem(), hbm(), hbm(), hbm(), hbm(), hbm()],
        out_specs=[vmem(), vmem(), vmem()],
        out_shape=[
            jax.ShapeDtypeStruct(residual.shape, F32),
            jax.ShapeDtypeStruct(half, BF),
            jax.ShapeDtypeStruct(half, BF),
        ],
        scratch_shapes=[
            pltpu.VMEM((steps, tokens, rows), BF),
            pltpu.VMEM((steps, tokens, cols), BF),
            pltpu.VMEM((steps, blocks, WIDTH), F32),
            pltpu.VMEM(in_count.shape, jnp.int32),
            pltpu.VMEM(in_rank.shape, jnp.int32),
            pltpu.VMEM((steps, blocks // WIDTH, WIDTH), jnp.int32),
            pltpu.VMEM((steps, WIDTH, WIDTH), F32),
            pltpu.SemaphoreType.DMA((2 + 2 * steps + blocks // PART,)),
        ],
        compiler_params=params,
        name="local",
    )(core, *[pltpu.with_memory_space_constraint(v, pltpu.HBM)
            for v in (acts, cotangent, residual, in_count, in_rank)])

    given = other_core(give)
    new_residual = pl.pallas_call(
        store_kernel,
        in_specs=[vmem()],
        out_specs=hbm(),
        out_shape=jax.ShapeDtypeStruct(residual.shape, F32),
        scratch_shapes=[pltpu.SemaphoreType.DMA],
        compiler_params=params,
        name="store",
    )(new_resid)
    pair = (keep.astype(F32) + given.astype(F32)).astype(BF)
    pair, new_residual = lax.optimization_barrier((pair, new_residual))
    first = exchange(pair.reshape(NZ, NY, steps, REGION, WIDTH), lines((1,), (2,)))
    line = jnp.sum(first.astype(F32), axis=0).astype(BF)
    arrived = exchange(line, lines((2,), (1,)))

    tile = jax.ShapeDtypeStruct((REGION, WIDTH), F32)
    outgoing, last, kept = pl.pallas_call(
        owner_kernel,
        in_specs=[vmem(), vmem(), vmem(), vmem()],
        out_specs=[vmem(), vmem(), vmem()],
        out_shape=[jax.ShapeDtypeStruct((NX, steps, REGION, WIDTH), BF), tile, tile],
        compiler_params=params,
        name="owner",
    )(arrived, owner_residual, out_count, out_rank)

    copies = pl.pallas_call(
        update_kernel,
        in_specs=[vmem()],
        out_specs=vmem(),
        out_shape=jax.ShapeDtypeStruct((CHIPS, REGION, WIDTH), BF),
        compiler_params=params,
        name="update",
    )(exchange(outgoing, groups_along((0,))))
    halves = of_both_cores(exchange(copies, groups_along((1, 2))))
    applied, new_owner = pl.pallas_call(
        assemble_kernel,
        in_specs=[vmem(), vmem(), vmem()],
        out_specs=[vmem(), vmem()],
        out_shape=[
            jax.ShapeDtypeStruct((rows, cols), BF),
            jax.ShapeDtypeStruct(owner_residual.shape, F32),
        ],
        scratch_shapes=[
            pltpu.VMEM((blocks, WIDTH), F32),
        ],
        compiler_params=params,
        name="assemble",
    )(halves, last, kept)
    return applied, new_residual, new_owner


def solution(mesh):
    flat = Mesh(mesh.devices.reshape(-1), ("d",))
    spec = P("d")
    return jax.shard_map(
        per_device,
        mesh=flat,
        in_specs=(spec,) * 8,
        out_specs=(P(), spec, spec),
        check_vma=False,
    )
```

```python
import math

import jax
import jax.numpy as jnp
import numpy as np
from jax import lax
from jax.experimental import pallas as pl
from jax.experimental.pallas import tpu as pltpu
from jax.sharding import Mesh
from jax.sharding import PartitionSpec as P

STEP_SIZE = 0.0625
NX, NZ, NY, NC = 4, 8, 8, 2
CHIPS = NZ * NY
REGION = 16
WIDTH = 128
BF = jnp.bfloat16
F32 = jnp.float32
VMEM_LIMIT = 48 * 1024 * 1024


def groups_along(axes):
    ids = np.arange(NX * NZ * NY * NC).reshape(NX, NZ, NY, NC)
    size = int(np.prod([ids.shape[a] for a in axes]))
    return np.moveaxis(ids, axes, range(4 - len(axes), 4)).reshape(-1, size).tolist()


def exchange(value, axes):
    return lax.all_to_all(
        value, "d", split_axis=0, concat_axis=0, tiled=True, axis_index_groups=groups_along(axes)
    )


def other_core(value):
    pairs = [(i, i ^ 1) for i in range(NX * NZ * NY * NC)]
    return lax.ppermute(value, "d", pairs)


def of_both_cores(value):
    return lax.all_gather(value, "d", axis=0, axis_index_groups=groups_along((3,)))


def local_kernel(scale, core_ref, acts_hbm, cot_hbm, resid_hbm, count_hbm, rank_hbm,
                 resid_ref, keep_ref, give_ref,
                 acts_ref, cot_ref, acc_ref, count_ref, rank_ref, ranks_ref, chosen_ref, sems):
    core = core_ref[0]
    steps, _, rows = acts_ref.shape
    cols = cot_ref.shape[2]
    tiles = cols // WIDTH
    groups = resid_ref.shape[1] // WIDTH

    copies = [
        pltpu.make_async_copy(rank_hbm, rank_ref, sems.at[0]),
        pltpu.make_async_copy(count_hbm, count_ref, sems.at[1]),
        pltpu.make_async_copy(resid_hbm, resid_ref, sems.at[2]),
    ]
    for s in range(steps):
        copies.append(pltpu.make_async_copy(acts_hbm.at[0, s], acts_ref.at[s], sems.at[3 + 2 * s]))
        copies.append(pltpu.make_async_copy(cot_hbm.at[0, s], cot_ref.at[s], sems.at[4 + 2 * s]))
    for i in [0, 1, 3, 4, 2] + list(range(5, 3 + 2 * steps)):
        copies[i].start()

    per = WIDTH // groups
    row_id = lax.broadcasted_iota(jnp.int32, (groups, WIDTH), 0)
    lane_id = lax.broadcasted_iota(jnp.int32, (groups, WIDTH), 1)
    owner_id = lax.broadcasted_iota(jnp.int32, (WIDTH, WIDTH), 0) % per
    block_id = lax.broadcasted_iota(jnp.int32, (WIDTH, WIDTH), 1) // REGION
    place = jnp.where(owner_id == block_id, 1.0, 0.0).astype(BF)
    eye = jnp.where(row_id == lane_id, 1.0, 0.0).astype(BF)
    copies[0].wait()
    copies[1].wait()
    for s in range(steps):
        for r in range(groups):
            ranks_ref[s, r:r + 1, :] = rank_ref[0, s:s + 1, r * WIDTH:(r + 1) * WIDTH]
        count = jnp.broadcast_to(count_ref[0, s:s + 1, :].astype(F32), (groups, WIDTH))
        spread = jnp.where(lane_id // per == row_id, count, 0.0)
        limit = jnp.dot(spread.astype(BF), place, preferred_element_type=F32)
        chosen = jnp.where(ranks_ref[s].astype(F32) < limit, 1.0, 0.0)
        chosen_ref[s] = lax.dot_general(chosen.astype(BF), eye, (((0,), (0,)), ((), ())),
                                        preferred_element_type=F32)

    half = 2 * WIDTH
    for s in range(steps):
        copies[3 + 2 * s].wait()
        copies[4 + 2 * s].wait()
        left = acts_ref[s]
        for h in range(cols // half):
            grad = lax.dot_general(left, cot_ref[s, :, h * half:(h + 1) * half],
                                   (((0,), (0,)), ((), ())), preferred_element_type=F32)
            grad = grad * scale
            for q in range(2):
                acc_ref[pl.ds(2 * h + q, rows, stride=tiles), :] = grad[:, q * WIDTH:(q + 1) * WIDTH]
        if s == 0:
            copies[2].wait()
        columns = chosen_ref[s]
        for me in range(NC):
            @pl.when(core == me)
            def _(me=me, s=s, columns=columns):
                for r in range(groups):
                    span = slice(r * WIDTH, (r + 1) * WIDTH)
                    total = resid_ref[0, span, :] + acc_ref[span, :]
                    mask = jnp.broadcast_to(columns[:, r:r + 1], (WIDTH, WIDTH)) > 0.5
                    resid_ref[0, span, :] = jnp.where(mask, 0.0, total)
                    sent = jnp.where(mask, total, 0.0).astype(BF)
                    for i in range(WIDTH // REGION):
                        owner = r * (WIDTH // REGION) + i
                        to = keep_ref if owner % NC == me else give_ref
                        to[owner // NC, s] = sent[i * REGION:(i + 1) * REGION, :]


def store_kernel(value_ref, out_hbm, sem):
    copy = pltpu.make_async_copy(value_ref, out_hbm, sem)
    copy.start()
    copy.wait()


def owner_kernel(arrived_ref, oresid_ref, count_ref, rank_ref, out_ref, last_ref, kept_ref):
    eye = (lax.broadcasted_iota(jnp.int32, (REGION, REGION), 0)
           == lax.broadcasted_iota(jnp.int32, (REGION, REGION), 1))
    oresid = oresid_ref[0]
    for s in range(rank_ref.shape[1]):
        total = arrived_ref[0, s].astype(F32)
        for k in range(1, arrived_ref.shape[0]):
            total = total + arrived_ref[k, s].astype(F32)
        count = jnp.broadcast_to(count_ref[0:1, s:s + 1], (1, REGION))
        row = jnp.where(rank_ref[0, s:s + 1, :] < count, 1.0, 0.0)
        square = jnp.where(eye, jnp.broadcast_to(row, (REGION, REGION)), 0.0)
        passed = jnp.broadcast_to(jnp.sum(square, axis=1, keepdims=True), (REGION, WIDTH)) > 0.5
        total = total + oresid
        going = jnp.where(passed, total, 0.0).astype(BF)
        oresid = jnp.where(passed, 0.0, total)
        for k in range(out_ref.shape[0]):
            out_ref[k, s] = going
    last_ref[...] = total
    kept_ref[...] = jnp.where(passed, 0.0, 1.0)


def update_kernel(arrived_ref, out_ref):
    total = jnp.zeros((REGION, WIDTH), F32)
    for s in range(arrived_ref.shape[1]):
        cross = arrived_ref[0, s].astype(F32)
        for x in range(1, NX):
            cross = cross + arrived_ref[x, s].astype(F32)
        total = total + cross.astype(BF).astype(F32)
    applied = (-STEP_SIZE * total).astype(BF)
    for k in range(out_ref.shape[0]):
        out_ref[k] = applied


def assemble_kernel(halves_ref, last_ref, kept_ref, out_ref, oresid_ref, flat_ref):
    oresid_ref[0] = jnp.where(kept_ref[...] > 0.5, last_ref[...], 0.0)
    rows, cols = out_ref.shape
    tiles = cols // WIDTH
    for i in range(CHIPS):
        for c in range(NC):
            at = (i * NC + c) * REGION
            flat_ref[at:at + REGION, :] = halves_ref[c, i].astype(F32)
    for t in range(tiles):
        out_ref[:, t * WIDTH:(t + 1) * WIDTH] = flat_ref[pl.ds(t, rows, stride=tiles), :].astype(BF)


def vmem():
    return pl.BlockSpec(memory_space=pltpu.VMEM)


def hbm():
    return pl.BlockSpec(memory_space=pltpu.HBM)


def smem():
    return pl.BlockSpec(memory_space=pltpu.SMEM)


def per_device(acts, cotangent, residual, owner_residual, in_count, in_rank, out_count, out_rank):
    steps, tokens, rows = acts.shape[1:]
    cols = cotangent.shape[3]
    blocks = residual.shape[1]
    scale = 1.0 / math.sqrt(tokens * CHIPS * NC)
    core = (lax.axis_index("d") % NC).astype(jnp.int32).reshape(1)
    params = pltpu.CompilerParams(vmem_limit_bytes=VMEM_LIMIT)

    def local(*args):
        return local_kernel(scale, *args)

    half = (CHIPS, steps, REGION, WIDTH)
    new_resid, keep, give = pl.pallas_call(
        local,
        in_specs=[smem(), hbm(), hbm(), hbm(), hbm(), hbm()],
        out_specs=[vmem(), vmem(), vmem()],
        out_shape=[
            jax.ShapeDtypeStruct(residual.shape, F32),
            jax.ShapeDtypeStruct(half, BF),
            jax.ShapeDtypeStruct(half, BF),
        ],
        scratch_shapes=[
            pltpu.VMEM((steps, tokens, rows), BF),
            pltpu.VMEM((steps, tokens, cols), BF),
            pltpu.VMEM((blocks, WIDTH), F32),
            pltpu.VMEM(in_count.shape, jnp.int32),
            pltpu.VMEM(in_rank.shape, jnp.int32),
            pltpu.VMEM((steps, blocks // WIDTH, WIDTH), jnp.int32),
            pltpu.VMEM((steps, WIDTH, WIDTH), F32),
            pltpu.SemaphoreType.DMA((3 + 2 * steps,)),
        ],
        compiler_params=params,
        name="local",
    )(core, *[pltpu.with_memory_space_constraint(v, pltpu.HBM)
            for v in (acts, cotangent, residual, in_count, in_rank)])

    given = other_core(give)
    new_residual = pl.pallas_call(
        store_kernel,
        in_specs=[vmem()],
        out_specs=hbm(),
        out_shape=jax.ShapeDtypeStruct(residual.shape, F32),
        scratch_shapes=[pltpu.SemaphoreType.DMA],
        compiler_params=params,
        name="store",
    )(new_resid)
    pair = (keep.astype(F32) + given.astype(F32)).astype(BF)
    pair, new_residual = lax.optimization_barrier((pair, new_residual))
    arrived = exchange(pair, (1, 2))

    tile = jax.ShapeDtypeStruct((REGION, WIDTH), F32)
    outgoing, last, kept = pl.pallas_call(
        owner_kernel,
        in_specs=[vmem(), vmem(), vmem(), vmem()],
        out_specs=[vmem(), vmem(), vmem()],
        out_shape=[jax.ShapeDtypeStruct((NX, steps, REGION, WIDTH), BF), tile, tile],
        compiler_params=params,
        name="owner",
    )(arrived, owner_residual, out_count, out_rank)

    copies = pl.pallas_call(
        update_kernel,
        in_specs=[vmem()],
        out_specs=vmem(),
        out_shape=jax.ShapeDtypeStruct((CHIPS, REGION, WIDTH), BF),
        compiler_params=params,
        name="update",
    )(exchange(outgoing, (0,)))
    halves = of_both_cores(exchange(copies, (1, 2)))
    applied, new_owner = pl.pallas_call(
        assemble_kernel,
        in_specs=[vmem(), vmem(), vmem()],
        out_specs=[vmem(), vmem()],
        out_shape=[
            jax.ShapeDtypeStruct((rows, cols), BF),
            jax.ShapeDtypeStruct(owner_residual.shape, F32),
        ],
        scratch_shapes=[
            pltpu.VMEM((blocks, WIDTH), F32),
        ],
        compiler_params=params,
        name="assemble",
    )(halves, last, kept)
    return applied, new_residual, new_owner


def solution(mesh):
    flat = Mesh(mesh.devices.reshape(-1), ("d",))
    spec = P("d")
    return jax.shard_map(
        per_device,
        mesh=flat,
        in_specs=(spec,) * 8,
        out_specs=(P(), spec, spec),
        check_vma=False,
    )
```

```python
import math

import jax
import jax.numpy as jnp
import numpy as np
from jax import lax
from jax.experimental import pallas as pl
from jax.experimental.pallas import tpu as pltpu
from jax.sharding import Mesh
from jax.sharding import PartitionSpec as P

STEP_SIZE = 0.0625
NX, NZ, NY, NC = 4, 8, 8, 2
CHIPS = NZ * NY
REGION = 16
ROWS = 4
WIDTH = 128
BF = jnp.bfloat16
F32 = jnp.float32
VMEM_LIMIT = 48 * 1024 * 1024


def groups_along(axes):
    ids = np.arange(NX * NZ * NY * NC).reshape(NX, NZ, NY, NC)
    size = int(np.prod([ids.shape[a] for a in axes]))
    return np.moveaxis(ids, axes, range(4 - len(axes), 4)).reshape(-1, size).tolist()


def exchange(value, axes):
    return lax.all_to_all(
        value, "d", split_axis=0, concat_axis=0, tiled=True, axis_index_groups=groups_along(axes)
    )


def other_core(value):
    pairs = [(i, i ^ 1) for i in range(NX * NZ * NY * NC)]
    return lax.ppermute(value, "d", pairs)


def of_both_cores(value):
    return lax.all_gather(value, "d", axis=0, axis_index_groups=groups_along((3,)))


def local_kernel(scale, core_ref, acts_hbm, cot_hbm, resid_hbm, count_hbm, rank_hbm,
                 resid_ref, keep_ref, give_ref,
                 acts_ref, cot_ref, acc_ref, count_ref, rank_ref, ranks_ref, chosen_ref, sems):
    core = core_ref[0]
    steps, _, rows = acts_ref.shape
    cols = cot_ref.shape[2]
    tiles = cols // WIDTH
    groups = resid_ref.shape[1] // WIDTH

    copies = [
        pltpu.make_async_copy(rank_hbm, rank_ref, sems.at[0]),
        pltpu.make_async_copy(count_hbm, count_ref, sems.at[1]),
        pltpu.make_async_copy(resid_hbm, resid_ref, sems.at[2]),
    ]
    for s in range(steps):
        copies.append(pltpu.make_async_copy(acts_hbm.at[0, s], acts_ref.at[s], sems.at[3 + 2 * s]))
        copies.append(pltpu.make_async_copy(cot_hbm.at[0, s], cot_ref.at[s], sems.at[4 + 2 * s]))
    for i in [0, 1, 3, 4, 2] + list(range(5, 3 + 2 * steps)):
        copies[i].start()

    per = WIDTH // groups
    row_id = lax.broadcasted_iota(jnp.int32, (groups, WIDTH), 0)
    lane_id = lax.broadcasted_iota(jnp.int32, (groups, WIDTH), 1)
    owner_id = lax.broadcasted_iota(jnp.int32, (WIDTH, WIDTH), 0) % per
    block_id = lax.broadcasted_iota(jnp.int32, (WIDTH, WIDTH), 1) // REGION
    place = jnp.where(owner_id == block_id, 1.0, 0.0).astype(BF)
    eye = jnp.where(row_id == lane_id, 1.0, 0.0).astype(BF)
    copies[0].wait()
    copies[1].wait()
    for s in range(steps):
        for r in range(groups):
            ranks_ref[s, r:r + 1, :] = rank_ref[0, s:s + 1, r * WIDTH:(r + 1) * WIDTH]
        count = jnp.broadcast_to(count_ref[0, s:s + 1, :].astype(F32), (groups, WIDTH))
        spread = jnp.where(lane_id // per == row_id, count, 0.0)
        limit = jnp.dot(spread.astype(BF), place, preferred_element_type=F32)
        chosen = jnp.where(ranks_ref[s].astype(F32) < limit, 1.0, 0.0)
        chosen_ref[s] = lax.dot_general(chosen.astype(BF), eye, (((0,), (0,)), ((), ())),
                                        preferred_element_type=F32)

    half = 2 * WIDTH
    for s in range(steps):
        copies[3 + 2 * s].wait()
        copies[4 + 2 * s].wait()
        left = acts_ref[s]
        for h in range(cols // half):
            grad = lax.dot_general(left, cot_ref[s, :, h * half:(h + 1) * half],
                                   (((0,), (0,)), ((), ())), preferred_element_type=F32)
            grad = grad * scale
            for q in range(2):
                acc_ref[pl.ds(2 * h + q, rows, stride=tiles), :] = grad[:, q * WIDTH:(q + 1) * WIDTH]
        if s == 0:
            copies[2].wait()
        columns = chosen_ref[s]
        for me in range(NC):
            @pl.when(core == me)
            def _(me=me, s=s, columns=columns):
                for r in range(groups):
                    span = slice(r * WIDTH, (r + 1) * WIDTH)
                    total = resid_ref[0, span, :] + acc_ref[span, :]
                    mask = jnp.broadcast_to(columns[:, r:r + 1], (WIDTH, WIDTH)) > 0.5
                    resid_ref[0, span, :] = jnp.where(mask, 0.0, total)
                    sent = jnp.where(mask, total, 0.0).astype(BF)
                    for i in range(WIDTH // REGION):
                        owner = r * (WIDTH // REGION) + i
                        to = keep_ref if owner % NC == me else give_ref
                        to[owner // NC, s] = sent[i * REGION:(i + 1) * REGION, :]


def store_kernel(value_ref, out_hbm, sem):
    copy = pltpu.make_async_copy(value_ref, out_hbm, sem)
    copy.start()
    copy.wait()


def owner_kernel(arrived_ref, oresid_ref, count_ref, rank_ref, out_ref, last_ref, kept_ref, going_ref):
    eye = (lax.broadcasted_iota(jnp.int32, (REGION, REGION), 0)
           == lax.broadcasted_iota(jnp.int32, (REGION, REGION), 1))
    oresid = oresid_ref[0]
    for s in range(rank_ref.shape[1]):
        total = arrived_ref[0, s].astype(F32)
        for k in range(1, arrived_ref.shape[0]):
            total = total + arrived_ref[k, s].astype(F32)
        count = jnp.broadcast_to(count_ref[0:1, s:s + 1], (1, REGION))
        row = jnp.where(rank_ref[0, s:s + 1, :] < count, 1.0, 0.0)
        square = jnp.where(eye, jnp.broadcast_to(row, (REGION, REGION)), 0.0)
        passed = jnp.broadcast_to(jnp.sum(square, axis=1, keepdims=True), (REGION, WIDTH)) > 0.5
        total = total + oresid
        going_ref[s] = jnp.where(passed, total, 0.0)
        oresid = jnp.where(passed, 0.0, total)
        for c in range(NC):
            tiles = [going_ref[s, pl.ds(NC * c + j, ROWS, stride=REGION // ROWS), :] for j in range(2)]
            both = jnp.concatenate(tiles, axis=0).astype(BF)
            for x in range(NX):
                out_ref[x * NC + c, s] = both
    last_ref[...] = total
    kept_ref[...] = jnp.where(passed, 0.0, 1.0)


def update_kernel(arrived_ref, out_ref):
    parts = []
    for c in range(NC):
        total = jnp.zeros(arrived_ref.shape[2:], F32)
        for s in range(arrived_ref.shape[1]):
            cross = arrived_ref[c, s].astype(F32)
            for x in range(1, NX):
                cross = cross + arrived_ref[x * NC + c, s].astype(F32)
            total = total + cross.astype(BF).astype(F32)
        parts.append(-STEP_SIZE * total)
    for j in range(2):
        tile = jnp.concatenate([part[j * ROWS:(j + 1) * ROWS] for part in parts], axis=0).astype(BF)
        for k in range(out_ref.shape[0]):
            out_ref[k, j] = tile


def assemble_kernel(halves_ref, last_ref, kept_ref, out_hbm, oresid_ref, sems):
    sends = []
    for c in range(NC):
        for j in range(2):
            t = 2 * c + j
            sends.append(pltpu.make_async_copy(
                halves_ref.at[c, :, j], out_hbm.at[:, :, t * WIDTH:(t + 1) * WIDTH], sems.at[t]))
            sends[-1].start()
    oresid_ref[0] = jnp.where(kept_ref[...] > 0.5, last_ref[...], 0.0)
    for send in sends:
        send.wait()


def vmem():
    return pl.BlockSpec(memory_space=pltpu.VMEM)


def hbm():
    return pl.BlockSpec(memory_space=pltpu.HBM)


def smem():
    return pl.BlockSpec(memory_space=pltpu.SMEM)


def per_device(acts, cotangent, residual, owner_residual, in_count, in_rank, out_count, out_rank):
    steps, tokens, rows = acts.shape[1:]
    cols = cotangent.shape[3]
    blocks = residual.shape[1]
    scale = 1.0 / math.sqrt(tokens * CHIPS * NC)
    core = (lax.axis_index("d") % NC).astype(jnp.int32).reshape(1)
    params = pltpu.CompilerParams(vmem_limit_bytes=VMEM_LIMIT)

    def local(*args):
        return local_kernel(scale, *args)

    half = (CHIPS, steps, REGION, WIDTH)
    new_resid, keep, give = pl.pallas_call(
        local,
        in_specs=[smem(), hbm(), hbm(), hbm(), hbm(), hbm()],
        out_specs=[vmem(), vmem(), vmem()],
        out_shape=[
            jax.ShapeDtypeStruct(residual.shape, F32),
            jax.ShapeDtypeStruct(half, BF),
            jax.ShapeDtypeStruct(half, BF),
        ],
        scratch_shapes=[
            pltpu.VMEM((steps, tokens, rows), BF),
            pltpu.VMEM((steps, tokens, cols), BF),
            pltpu.VMEM((blocks, WIDTH), F32),
            pltpu.VMEM(in_count.shape, jnp.int32),
            pltpu.VMEM(in_rank.shape, jnp.int32),
            pltpu.VMEM((steps, blocks // WIDTH, WIDTH), jnp.int32),
            pltpu.VMEM((steps, WIDTH, WIDTH), F32),
            pltpu.SemaphoreType.DMA((3 + 2 * steps,)),
        ],
        compiler_params=params,
        name="local",
    )(core, *[pltpu.with_memory_space_constraint(v, pltpu.HBM)
            for v in (acts, cotangent, residual, in_count, in_rank)])

    given = other_core(give)
    new_residual = pl.pallas_call(
        store_kernel,
        in_specs=[vmem()],
        out_specs=hbm(),
        out_shape=jax.ShapeDtypeStruct(residual.shape, F32),
        scratch_shapes=[pltpu.SemaphoreType.DMA],
        compiler_params=params,
        name="store",
    )(new_resid)
    pair = (keep.astype(F32) + given.astype(F32)).astype(BF)
    pair, new_residual = lax.optimization_barrier((pair, new_residual))
    arrived = exchange(pair, (1, 2))

    tile = jax.ShapeDtypeStruct((REGION, WIDTH), F32)
    outgoing, last, kept = pl.pallas_call(
        owner_kernel,
        in_specs=[vmem(), vmem(), vmem(), vmem()],
        out_specs=[vmem(), vmem(), vmem()],
        out_shape=[jax.ShapeDtypeStruct((NX * NC, steps, NC * ROWS, WIDTH), BF), tile, tile],
        scratch_shapes=[pltpu.VMEM((steps, REGION, WIDTH), F32)],
        compiler_params=params,
        name="owner",
    )(arrived, owner_residual, out_count, out_rank)

    copies = pl.pallas_call(
        update_kernel,
        in_specs=[vmem()],
        out_specs=vmem(),
        out_shape=jax.ShapeDtypeStruct((CHIPS, 2, NC * ROWS, WIDTH), BF),
        compiler_params=params,
        name="update",
    )(exchange(outgoing, (0, 3)))
    halves = of_both_cores(exchange(copies, (1, 2)))
    applied, new_owner = pl.pallas_call(
        assemble_kernel,
        in_specs=[vmem(), vmem(), vmem()],
        out_specs=[hbm(), vmem()],
        out_shape=[
            jax.ShapeDtypeStruct((CHIPS, NC * ROWS, cols), BF),
            jax.ShapeDtypeStruct(owner_residual.shape, F32),
        ],
        scratch_shapes=[pltpu.SemaphoreType.DMA((4,))],
        compiler_params=params,
        name="assemble",
    )(halves, last, kept)
    return applied.reshape(rows, cols), new_residual, new_owner


def solution(mesh):
    flat = Mesh(mesh.devices.reshape(-1), ("d",))
    spec = P("d")
    return jax.shard_map(
        per_device,
        mesh=flat,
        in_specs=(spec,) * 8,
        out_specs=(P(), spec, spec),
        check_vma=False,
    )
```

```python
import math

import jax
import jax.numpy as jnp
import numpy as np
from jax import lax
from jax.experimental import pallas as pl
from jax.experimental.pallas import tpu as pltpu
from jax.sharding import Mesh
from jax.sharding import PartitionSpec as P

STEP_SIZE = 0.0625
NX, NZ, NY, NC = 4, 8, 8, 2
CHIPS = NZ * NY
REGION = 16
CAP = 8
NONE = 31.0
WHOLE = (NZ * NY * 2 - 1) * REGION
WIDTH = 128
BF = jnp.bfloat16
F32 = jnp.float32
VMEM_LIMIT = 48 * 1024 * 1024


def groups_along(axes):
    ids = np.arange(NX * NZ * NY * NC).reshape(NX, NZ, NY, NC)
    size = int(np.prod([ids.shape[a] for a in axes]))
    return np.moveaxis(ids, axes, range(4 - len(axes), 4)).reshape(-1, size).tolist()


def exchange(value, axes):
    return lax.all_to_all(
        value, "d", split_axis=0, concat_axis=0, tiled=True, axis_index_groups=groups_along(axes)
    )


def of_both_cores(value):
    return lax.all_gather(value, "d", axis=0, axis_index_groups=groups_along((3,)))


def local_kernel(scale, core_ref, acts_hbm, cot_hbm, resid_hbm, count_hbm, rank_hbm,
                 resid_ref, keep_ref, give_ref,
                 acts_ref, cot_ref, acc_ref, count_ref, rank_ref, ranks_ref, chosen_ref, last_ref, pack_ref, sems):
    core = core_ref[0]
    steps, _, rows = acts_ref.shape
    cols = cot_ref.shape[2]
    tiles = cols // WIDTH
    groups = resid_ref.shape[1] // WIDTH

    copies = [
        pltpu.make_async_copy(rank_hbm, rank_ref, sems.at[0]),
        pltpu.make_async_copy(count_hbm, count_ref, sems.at[1]),
        pltpu.make_async_copy(resid_hbm, resid_ref, sems.at[2]),
    ]
    for s in range(steps):
        copies.append(pltpu.make_async_copy(acts_hbm.at[0, s], acts_ref.at[s], sems.at[3 + 2 * s]))
        copies.append(pltpu.make_async_copy(cot_hbm.at[0, s], cot_ref.at[s], sems.at[4 + 2 * s]))
    for i in [0, 1, 3, 4, 2] + list(range(5, 3 + 2 * steps)):
        copies[i].start()

    per = WIDTH // groups
    row_id = lax.broadcasted_iota(jnp.int32, (groups, WIDTH), 0)
    lane_id = lax.broadcasted_iota(jnp.int32, (groups, WIDTH), 1)
    owner_id = lax.broadcasted_iota(jnp.int32, (WIDTH, WIDTH), 0) % per
    block_id = lax.broadcasted_iota(jnp.int32, (WIDTH, WIDTH), 1) // REGION
    place = jnp.where(owner_id == block_id, 1.0, 0.0).astype(BF)
    eye = jnp.where(row_id == lane_id, 1.0, 0.0).astype(BF)
    copies[0].wait()
    copies[1].wait()
    for s in range(steps):
        for r in range(groups):
            ranks_ref[s, r:r + 1, :] = rank_ref[0, s:s + 1, r * WIDTH:(r + 1) * WIDTH]
        count = jnp.broadcast_to(count_ref[0, s:s + 1, :].astype(F32), (groups, WIDTH))
        spread = jnp.where(lane_id // per == row_id, count, 0.0)
        limit = jnp.dot(spread.astype(BF), place, preferred_element_type=F32)
        chosen = jnp.where(ranks_ref[s].astype(F32) < limit, 1.0, 0.0)
        if s == steps - 1:
            last_ref[...] = jnp.where(chosen > 0.5, ranks_ref[s].astype(F32), NONE)
        chosen_ref[s] = lax.dot_general(chosen.astype(BF), eye, (((0,), (0,)), ((), ())),
                                        preferred_element_type=F32)

    half = 2 * WIDTH
    for s in range(steps):
        copies[3 + 2 * s].wait()
        copies[4 + 2 * s].wait()
        left = acts_ref[s]
        for h in range(cols // half):
            grad = lax.dot_general(left, cot_ref[s, :, h * half:(h + 1) * half],
                                   (((0,), (0,)), ((), ())), preferred_element_type=F32)
            grad = grad * scale
            for q in range(2):
                acc_ref[pl.ds(2 * h + q, rows, stride=tiles), :] = grad[:, q * WIDTH:(q + 1) * WIDTH]
        if s == 0:
            copies[2].wait()
        columns = chosen_ref[s]
        for me in range(NC):
            @pl.when(core == me)
            def _(me=me, s=s, columns=columns):
                for r in range(groups):
                    span = slice(r * WIDTH, (r + 1) * WIDTH)
                    total = resid_ref[0, span, :] + acc_ref[span, :]
                    mask = jnp.broadcast_to(columns[:, r:r + 1], (WIDTH, WIDTH)) > 0.5
                    resid_ref[0, span, :] = jnp.where(mask, 0.0, total)
                    sent = jnp.where(mask, total, 0.0).astype(BF)
                    for i in range(WIDTH // REGION):
                        owner = r * (WIDTH // REGION) + i
                        at = ((owner // NC) * steps + s) * REGION
                        tile = sent[i * REGION:(i + 1) * REGION, :]
                        if owner % NC == me:
                            keep_ref[at:at + REGION, :] = tile
                        elif at < WHOLE:
                            give_ref[at:at + REGION, :] = tile
                        else:
                            slots = last_ref[r:r + 1, :]
                            wide = jnp.broadcast_to(slots, (REGION, WIDTH))
                            slot = lax.broadcasted_iota(jnp.int32, (REGION, WIDTH), 0).astype(F32)
                            lane = lax.broadcasted_iota(jnp.int32, (REGION, WIDTH), 1)
                            pick = jnp.where((wide == slot) & (lane // REGION == i), 1.0, 0.0)
                            packed = jnp.dot(pick.astype(BF), sent, preferred_element_type=F32)
                            pack_ref[0:CAP, :] = packed[0:CAP, :]
                            pack_ref[CAP:2 * CAP, :] = jnp.broadcast_to(slots, (CAP, WIDTH))
                            give_ref[at:at + CAP + 2, :] = pack_ref[0:CAP + 2, :].astype(BF)


def pair_kernel(core_ref, keep_ref, both_ref, out_ref, tile_ref):
    core = core_ref[0]
    other = 1 - core
    chunk = 8 * REGION
    for at in range(0, WHOLE, chunk):
        span = slice(at, min(at + chunk, WHOLE))
        total = keep_ref[span, :].astype(F32) + both_ref[other, span, :].astype(F32)
        out_ref[span, :] = total.astype(BF)
    packed = both_ref[other, WHOLE:WHOLE + CAP, :].astype(F32)
    packed = jnp.concatenate([packed, jnp.zeros_like(packed)], axis=0).astype(BF)
    slots = both_ref[other, WHOLE + CAP:WHOLE + CAP + 2, :].astype(F32)[0:1, :]
    slot = lax.broadcasted_iota(jnp.int32, (REGION, WIDTH), 0).astype(F32)
    pick = jnp.where(jnp.broadcast_to(slots, (REGION, WIDTH)) == slot, 1.0, 0.0).astype(BF)
    tile_ref[...] = lax.dot_general(pick, packed, (((0,), (0,)), ((), ())), preferred_element_type=F32)
    at = pl.multiple_of(WIDTH - NC * REGION + core * REGION, REGION)
    total = keep_ref[WHOLE:WHOLE + REGION, :].astype(F32) + tile_ref[pl.ds(at, REGION), :]
    out_ref[WHOLE:WHOLE + REGION, :] = total.astype(BF)


def owner_kernel(arrived_ref, oresid_ref, count_ref, rank_ref, out_ref, last_ref, kept_ref):
    eye = (lax.broadcasted_iota(jnp.int32, (REGION, REGION), 0)
           == lax.broadcasted_iota(jnp.int32, (REGION, REGION), 1))
    oresid = oresid_ref[0]
    for s in range(rank_ref.shape[1]):
        total = arrived_ref[0, s].astype(F32)
        for k in range(1, arrived_ref.shape[0]):
            total = total + arrived_ref[k, s].astype(F32)
        count = jnp.broadcast_to(count_ref[0:1, s:s + 1], (1, REGION))
        row = jnp.where(rank_ref[0, s:s + 1, :] < count, 1.0, 0.0)
        square = jnp.where(eye, jnp.broadcast_to(row, (REGION, REGION)), 0.0)
        passed = jnp.broadcast_to(jnp.sum(square, axis=1, keepdims=True), (REGION, WIDTH)) > 0.5
        total = total + oresid
        going = jnp.where(passed, total, 0.0).astype(BF)
        oresid = jnp.where(passed, 0.0, total)
        for k in range(out_ref.shape[0]):
            out_ref[k, s] = going
    last_ref[...] = total
    kept_ref[...] = jnp.where(passed, 0.0, 1.0)


def update_kernel(arrived_ref, out_ref):
    total = jnp.zeros((REGION, WIDTH), F32)
    for s in range(arrived_ref.shape[1]):
        cross = arrived_ref[0, s].astype(F32)
        for x in range(1, NX):
            cross = cross + arrived_ref[x, s].astype(F32)
        total = total + cross.astype(BF).astype(F32)
    applied = (-STEP_SIZE * total).astype(BF)
    for k in range(out_ref.shape[0]):
        out_ref[k] = applied


def assemble_kernel(halves_ref, last_ref, kept_ref, out_ref, oresid_ref, flat_ref):
    oresid_ref[0] = jnp.where(kept_ref[...] > 0.5, last_ref[...], 0.0)
    rows, cols = out_ref.shape
    tiles = cols // WIDTH
    for i in range(CHIPS):
        for c in range(NC):
            at = (i * NC + c) * REGION
            flat_ref[at:at + REGION, :] = halves_ref[c, i].astype(F32)
    for t in range(tiles):
        out_ref[:, t * WIDTH:(t + 1) * WIDTH] = flat_ref[pl.ds(t, rows, stride=tiles), :].astype(BF)


def vmem():
    return pl.BlockSpec(memory_space=pltpu.VMEM)


def hbm():
    return pl.BlockSpec(memory_space=pltpu.HBM)


def smem():
    return pl.BlockSpec(memory_space=pltpu.SMEM)


def per_device(acts, cotangent, residual, owner_residual, in_count, in_rank, out_count, out_rank):
    steps, tokens, rows = acts.shape[1:]
    cols = cotangent.shape[3]
    blocks = residual.shape[1]
    scale = 1.0 / math.sqrt(tokens * CHIPS * NC)
    core = (lax.axis_index("d") % NC).astype(jnp.int32).reshape(1)
    params = pltpu.CompilerParams(vmem_limit_bytes=VMEM_LIMIT)

    def local(*args):
        return local_kernel(scale, *args)

    size = CHIPS * steps * REGION
    new_resid, keep, give = pl.pallas_call(
        local,
        in_specs=[smem(), hbm(), hbm(), hbm(), hbm(), hbm()],
        out_specs=[vmem(), vmem(), vmem()],
        out_shape=[
            pltpu.VMEM(residual.shape, F32),
            jax.ShapeDtypeStruct((size, WIDTH), BF),
            jax.ShapeDtypeStruct((WHOLE + CAP + 2, WIDTH), BF),
        ],
        scratch_shapes=[
            pltpu.VMEM((steps, tokens, rows), BF),
            pltpu.VMEM((steps, tokens, cols), BF),
            pltpu.VMEM((blocks, WIDTH), F32),
            pltpu.VMEM(in_count.shape, jnp.int32),
            pltpu.VMEM(in_rank.shape, jnp.int32),
            pltpu.VMEM((steps, blocks // WIDTH, WIDTH), jnp.int32),
            pltpu.VMEM((steps, WIDTH, WIDTH), F32),
            pltpu.VMEM((blocks // WIDTH, WIDTH), F32),
            pltpu.VMEM((2 * CAP, WIDTH), F32),
            pltpu.SemaphoreType.DMA((3 + 2 * steps,)),
        ],
        compiler_params=params,
        name="local",
    )(core, *[pltpu.with_memory_space_constraint(v, pltpu.HBM)
            for v in (acts, cotangent, residual, in_count, in_rank)])

    pair = pl.pallas_call(
        pair_kernel,
        in_specs=[smem(), vmem(), vmem()],
        out_specs=vmem(),
        out_shape=jax.ShapeDtypeStruct((size, WIDTH), BF),
        scratch_shapes=[pltpu.VMEM((WIDTH, WIDTH), F32)],
        compiler_params=params,
        name="pair",
    )(core, keep, of_both_cores(give))
    new_residual = new_resid
    pair = pair.reshape(CHIPS, steps, REGION, WIDTH)
    arrived = exchange(pair, (1, 2))

    tile = jax.ShapeDtypeStruct((REGION, WIDTH), F32)
    outgoing, last, kept = pl.pallas_call(
        owner_kernel,
        in_specs=[vmem(), vmem(), vmem(), vmem()],
        out_specs=[vmem(), vmem(), vmem()],
        out_shape=[jax.ShapeDtypeStruct((NX, steps, REGION, WIDTH), BF), tile, tile],
        compiler_params=params,
        name="owner",
    )(arrived, owner_residual, out_count, out_rank)

    copies = pl.pallas_call(
        update_kernel,
        in_specs=[vmem()],
        out_specs=vmem(),
        out_shape=pltpu.VMEM((CHIPS, REGION, WIDTH), BF),
        compiler_params=params,
        name="update",
    )(exchange(outgoing, (0,)))
    halves = of_both_cores(exchange(copies, (1, 2)))
    applied, new_owner = pl.pallas_call(
        assemble_kernel,
        in_specs=[vmem(), vmem(), vmem()],
        out_specs=[vmem(), vmem()],
        out_shape=[
            jax.ShapeDtypeStruct((rows, cols), BF),
            jax.ShapeDtypeStruct(owner_residual.shape, F32),
        ],
        scratch_shapes=[
            pltpu.VMEM((blocks, WIDTH), F32),
        ],
        compiler_params=params,
        name="assemble",
    )(halves, last, kept)
    return applied, new_residual, new_owner


def solution(mesh):
    flat = Mesh(mesh.devices.reshape(-1), ("d",))
    spec = P("d")
    return jax.shard_map(
        per_device,
        mesh=flat,
        in_specs=(spec,) * 8,
        out_specs=(P(), spec, spec),
        check_vma=False,
    )
```

```python
import math

import jax
import jax.numpy as jnp
import numpy as np
from jax import lax
from jax.experimental import pallas as pl
from jax.experimental.pallas import tpu as pltpu
from jax.sharding import Mesh
from jax.sharding import PartitionSpec as P

STEP_SIZE = 0.0625
NX, NZ, NY, NC = 4, 8, 8, 2
CHIPS = NZ * NY
REGION = 16
CAP = 8
NONE = 31.0
WHOLE = (NZ * NY * 2 - 1) * REGION
WIDTH = 128
BF = jnp.bfloat16
F32 = jnp.float32
VMEM_LIMIT = 48 * 1024 * 1024


def groups_along(axes):
    ids = np.arange(NX * NZ * NY * NC).reshape(NX, NZ, NY, NC)
    size = int(np.prod([ids.shape[a] for a in axes]))
    return np.moveaxis(ids, axes, range(4 - len(axes), 4)).reshape(-1, size).tolist()


def exchange(value, axes):
    return lax.all_to_all(
        value, "d", split_axis=0, concat_axis=0, tiled=True, axis_index_groups=groups_along(axes)
    )


def of_both_cores(value):
    return lax.all_gather(value, "d", axis=0, axis_index_groups=groups_along((3,)))


def local_kernel(scale, core_ref, acts_hbm, cot_hbm, resid_hbm, count_hbm, rank_hbm,
                 resid_ref, keep_ref, give_ref,
                 acts_ref, cot_ref, acc_ref, count_ref, rank_ref, ranks_ref, chosen_ref, last_ref, pack_ref, sems):
    core = core_ref[0]
    steps, _, rows = acts_ref.shape
    cols = cot_ref.shape[2]
    tiles = cols // WIDTH
    groups = resid_ref.shape[1] // WIDTH

    copies = [
        pltpu.make_async_copy(rank_hbm, rank_ref, sems.at[0]),
        pltpu.make_async_copy(count_hbm, count_ref, sems.at[1]),
        pltpu.make_async_copy(resid_hbm, resid_ref, sems.at[2]),
    ]
    for s in range(steps):
        copies.append(pltpu.make_async_copy(acts_hbm.at[0, s], acts_ref.at[s], sems.at[3 + 2 * s]))
        copies.append(pltpu.make_async_copy(cot_hbm.at[0, s], cot_ref.at[s], sems.at[4 + 2 * s]))
    for i in [0, 1, 3, 4, 2] + list(range(5, 3 + 2 * steps)):
        copies[i].start()

    per = WIDTH // groups
    row_id = lax.broadcasted_iota(jnp.int32, (groups, WIDTH), 0)
    lane_id = lax.broadcasted_iota(jnp.int32, (groups, WIDTH), 1)
    owner_id = lax.broadcasted_iota(jnp.int32, (WIDTH, WIDTH), 0) % per
    block_id = lax.broadcasted_iota(jnp.int32, (WIDTH, WIDTH), 1) // REGION
    place = jnp.where(owner_id == block_id, 1.0, 0.0).astype(BF)
    eye = jnp.where(row_id == lane_id, 1.0, 0.0).astype(BF)
    copies[0].wait()
    copies[1].wait()
    for s in range(steps):
        for r in range(groups):
            ranks_ref[s, r:r + 1, :] = rank_ref[0, s:s + 1, r * WIDTH:(r + 1) * WIDTH]
        count = jnp.broadcast_to(count_ref[0, s:s + 1, :].astype(F32), (groups, WIDTH))
        spread = jnp.where(lane_id // per == row_id, count, 0.0)
        limit = jnp.dot(spread.astype(BF), place, preferred_element_type=F32)
        chosen = jnp.where(ranks_ref[s].astype(F32) < limit, 1.0, 0.0)
        if s == steps - 1:
            last_ref[...] = jnp.where(chosen > 0.5, ranks_ref[s].astype(F32), NONE)
        chosen_ref[s] = lax.dot_general(chosen.astype(BF), eye, (((0,), (0,)), ((), ())),
                                        preferred_element_type=F32)

    half = 2 * WIDTH
    for s in range(steps):
        copies[3 + 2 * s].wait()
        copies[4 + 2 * s].wait()
        left = acts_ref[s]
        for h in range(cols // half):
            grad = lax.dot_general(left, cot_ref[s, :, h * half:(h + 1) * half],
                                   (((0,), (0,)), ((), ())), preferred_element_type=F32)
            grad = grad * scale
            for q in range(2):
                acc_ref[pl.ds(2 * h + q, rows, stride=tiles), :] = grad[:, q * WIDTH:(q + 1) * WIDTH]
        if s == 0:
            copies[2].wait()
        columns = chosen_ref[s]
        for me in range(NC):
            @pl.when(core == me)
            def _(me=me, s=s, columns=columns):
                for r in range(groups):
                    span = slice(r * WIDTH, (r + 1) * WIDTH)
                    total = resid_ref[0, span, :] + acc_ref[span, :]
                    mask = jnp.broadcast_to(columns[:, r:r + 1], (WIDTH, WIDTH)) > 0.5
                    resid_ref[0, span, :] = jnp.where(mask, 0.0, total)
                    sent = jnp.where(mask, total, 0.0).astype(BF)
                    for i in range(WIDTH // REGION):
                        owner = r * (WIDTH // REGION) + i
                        at = ((owner // NC) * steps + s) * REGION
                        tile = sent[i * REGION:(i + 1) * REGION, :]
                        if owner % NC == me:
                            keep_ref[at:at + REGION, :] = tile
                        elif at < WHOLE:
                            give_ref[at:at + REGION, :] = tile
                        else:
                            slots = last_ref[r:r + 1, :]
                            wide = jnp.broadcast_to(slots, (REGION, WIDTH))
                            slot = lax.broadcasted_iota(jnp.int32, (REGION, WIDTH), 0).astype(F32)
                            lane = lax.broadcasted_iota(jnp.int32, (REGION, WIDTH), 1)
                            pick = jnp.where((wide == slot) & (lane // REGION == i), 1.0, 0.0)
                            packed = jnp.dot(pick.astype(BF), sent, preferred_element_type=F32)
                            pack_ref[0:CAP, :] = packed[0:CAP, :]
                            pack_ref[CAP:2 * CAP, :] = jnp.broadcast_to(slots, (CAP, WIDTH))
                            give_ref[at:at + CAP + 2, :] = pack_ref[0:CAP + 2, :].astype(BF)


def stored(resid_ref, store_hbm, sem, part):
    quarter = resid_ref.shape[1] // 4
    span = slice(part[0] * quarter, part[1] * quarter)
    copy = pltpu.make_async_copy(resid_ref.at[:, span], store_hbm.at[:, span], sem)
    copy.start()
    return copy


def pair_kernel(core_ref, keep_ref, both_ref, resid_ref, out_ref, store_hbm, tile_ref, sem):
    store = stored(resid_ref, store_hbm, sem, (0, 1))
    core = core_ref[0]
    other = 1 - core
    chunk = 8 * REGION
    for at in range(0, WHOLE, chunk):
        span = slice(at, min(at + chunk, WHOLE))
        total = keep_ref[span, :].astype(F32) + both_ref[other, span, :].astype(F32)
        out_ref[span, :] = total.astype(BF)
    packed = both_ref[other, WHOLE:WHOLE + CAP, :].astype(F32)
    packed = jnp.concatenate([packed, jnp.zeros_like(packed)], axis=0).astype(BF)
    slots = both_ref[other, WHOLE + CAP:WHOLE + CAP + 2, :].astype(F32)[0:1, :]
    slot = lax.broadcasted_iota(jnp.int32, (REGION, WIDTH), 0).astype(F32)
    pick = jnp.where(jnp.broadcast_to(slots, (REGION, WIDTH)) == slot, 1.0, 0.0).astype(BF)
    tile_ref[...] = lax.dot_general(pick, packed, (((0,), (0,)), ((), ())), preferred_element_type=F32)
    at = pl.multiple_of(WIDTH - NC * REGION + core * REGION, REGION)
    total = keep_ref[WHOLE:WHOLE + REGION, :].astype(F32) + tile_ref[pl.ds(at, REGION), :]
    out_ref[WHOLE:WHOLE + REGION, :] = total.astype(BF)
    store.wait()


def owner_kernel(arrived_ref, oresid_ref, count_ref, rank_ref, resid_ref, begun_hbm,
                 out_ref, last_ref, kept_ref, store_hbm, sem):
    store = stored(resid_ref, store_hbm, sem, (1, 2))
    eye = (lax.broadcasted_iota(jnp.int32, (REGION, REGION), 0)
           == lax.broadcasted_iota(jnp.int32, (REGION, REGION), 1))
    oresid = oresid_ref[0]
    for s in range(rank_ref.shape[1]):
        total = arrived_ref[0, s].astype(F32)
        for k in range(1, arrived_ref.shape[0]):
            total = total + arrived_ref[k, s].astype(F32)
        count = jnp.broadcast_to(count_ref[0:1, s:s + 1], (1, REGION))
        row = jnp.where(rank_ref[0, s:s + 1, :] < count, 1.0, 0.0)
        square = jnp.where(eye, jnp.broadcast_to(row, (REGION, REGION)), 0.0)
        passed = jnp.broadcast_to(jnp.sum(square, axis=1, keepdims=True), (REGION, WIDTH)) > 0.5
        total = total + oresid
        going = jnp.where(passed, total, 0.0).astype(BF)
        oresid = jnp.where(passed, 0.0, total)
        for k in range(out_ref.shape[0]):
            out_ref[k, s] = going
    last_ref[...] = total
    kept_ref[...] = jnp.where(passed, 0.0, 1.0)
    store.wait()


def update_kernel(arrived_ref, out_ref):
    total = jnp.zeros((REGION, WIDTH), F32)
    for s in range(arrived_ref.shape[1]):
        cross = arrived_ref[0, s].astype(F32)
        for x in range(1, NX):
            cross = cross + arrived_ref[x, s].astype(F32)
        total = total + cross.astype(BF).astype(F32)
    applied = (-STEP_SIZE * total).astype(BF)
    for k in range(out_ref.shape[0]):
        out_ref[k] = applied


def assemble_kernel(halves_ref, last_ref, kept_ref, resid_ref, begun_hbm,
                    out_ref, oresid_ref, store_hbm, flat_ref, sem):
    store = stored(resid_ref, store_hbm, sem, (2, 4))
    oresid_ref[0] = jnp.where(kept_ref[...] > 0.5, last_ref[...], 0.0)
    rows, cols = out_ref.shape
    tiles = cols // WIDTH
    for i in range(CHIPS):
        for c in range(NC):
            at = (i * NC + c) * REGION
            flat_ref[at:at + REGION, :] = halves_ref[c, i].astype(F32)
    for t in range(tiles):
        out_ref[:, t * WIDTH:(t + 1) * WIDTH] = flat_ref[pl.ds(t, rows, stride=tiles), :].astype(BF)
    store.wait()


def vmem():
    return pl.BlockSpec(memory_space=pltpu.VMEM)


def hbm():
    return pl.BlockSpec(memory_space=pltpu.HBM)


def smem():
    return pl.BlockSpec(memory_space=pltpu.SMEM)


def per_device(acts, cotangent, residual, owner_residual, in_count, in_rank, out_count, out_rank):
    steps, tokens, rows = acts.shape[1:]
    cols = cotangent.shape[3]
    blocks = residual.shape[1]
    scale = 1.0 / math.sqrt(tokens * CHIPS * NC)
    core = (lax.axis_index("d") % NC).astype(jnp.int32).reshape(1)
    params = pltpu.CompilerParams(vmem_limit_bytes=VMEM_LIMIT)

    def local(*args):
        return local_kernel(scale, *args)

    size = CHIPS * steps * REGION
    new_resid, keep, give = pl.pallas_call(
        local,
        in_specs=[smem(), hbm(), hbm(), hbm(), hbm(), hbm()],
        out_specs=[vmem(), vmem(), vmem()],
        out_shape=[
            pltpu.VMEM(residual.shape, F32),
            jax.ShapeDtypeStruct((size, WIDTH), BF),
            jax.ShapeDtypeStruct((WHOLE + CAP + 2, WIDTH), BF),
        ],
        scratch_shapes=[
            pltpu.VMEM((steps, tokens, rows), BF),
            pltpu.VMEM((steps, tokens, cols), BF),
            pltpu.VMEM((blocks, WIDTH), F32),
            pltpu.VMEM(in_count.shape, jnp.int32),
            pltpu.VMEM(in_rank.shape, jnp.int32),
            pltpu.VMEM((steps, blocks // WIDTH, WIDTH), jnp.int32),
            pltpu.VMEM((steps, WIDTH, WIDTH), F32),
            pltpu.VMEM((blocks // WIDTH, WIDTH), F32),
            pltpu.VMEM((2 * CAP, WIDTH), F32),
            pltpu.SemaphoreType.DMA((3 + 2 * steps,)),
        ],
        compiler_params=params,
        name="local",
    )(core, *[pltpu.with_memory_space_constraint(v, pltpu.HBM)
            for v in (acts, cotangent, residual, in_count, in_rank)])

    placed = jax.ShapeDtypeStruct(residual.shape, F32)
    pair, store = pl.pallas_call(
        pair_kernel,
        in_specs=[smem(), vmem(), vmem(), vmem()],
        out_specs=[vmem(), hbm()],
        out_shape=[jax.ShapeDtypeStruct((size, WIDTH), BF), placed],
        scratch_shapes=[pltpu.VMEM((WIDTH, WIDTH), F32), pltpu.SemaphoreType.DMA],
        compiler_params=params,
        name="pair",
    )(core, keep, of_both_cores(give), new_resid)
    arrived = exchange(pair.reshape(CHIPS, steps, REGION, WIDTH), (1, 2))

    tile = jax.ShapeDtypeStruct((REGION, WIDTH), F32)
    outgoing, last, kept, store = pl.pallas_call(
        owner_kernel,
        in_specs=[vmem(), vmem(), vmem(), vmem(), vmem(), hbm()],
        out_specs=[vmem(), vmem(), vmem(), hbm()],
        out_shape=[jax.ShapeDtypeStruct((NX, steps, REGION, WIDTH), BF), tile, tile, placed],
        scratch_shapes=[pltpu.SemaphoreType.DMA],
        input_output_aliases={5: 3},
        compiler_params=params,
        name="owner",
    )(arrived, owner_residual, out_count, out_rank, new_resid, store)

    copies = pl.pallas_call(
        update_kernel,
        in_specs=[vmem()],
        out_specs=vmem(),
        out_shape=jax.ShapeDtypeStruct((CHIPS, REGION, WIDTH), BF),
        compiler_params=params,
        name="update",
    )(exchange(outgoing, (0,)))
    halves = of_both_cores(exchange(copies, (1, 2)))
    applied, new_owner, new_residual = pl.pallas_call(
        assemble_kernel,
        in_specs=[vmem(), vmem(), vmem(), vmem(), hbm()],
        out_specs=[vmem(), vmem(), hbm()],
        out_shape=[
            jax.ShapeDtypeStruct((rows, cols), BF),
            jax.ShapeDtypeStruct(owner_residual.shape, F32),
            placed,
        ],
        scratch_shapes=[pltpu.VMEM((blocks, WIDTH), F32), pltpu.SemaphoreType.DMA],
        input_output_aliases={4: 2},
        compiler_params=params,
        name="assemble",
    )(halves, last, kept, new_resid, store)
    return applied, new_residual, new_owner


def solution(mesh):
    flat = Mesh(mesh.devices.reshape(-1), ("d",))
    spec = P("d")
    return jax.shard_map(
        per_device,
        mesh=flat,
        in_specs=(spec,) * 8,
        out_specs=(P(), spec, spec),
        check_vma=False,
    )
```

```python
import math

import jax
import jax.numpy as jnp
import numpy as np
from jax import lax
from jax.experimental import pallas as pl
from jax.experimental.pallas import tpu as pltpu
from jax.sharding import Mesh
from jax.sharding import PartitionSpec as P

STEP_SIZE = 0.0625
NX, NZ, NY, NC = 4, 8, 8, 2
CHIPS = NZ * NY
REGION = 16
CAP = 8
NONE = 31.0
WHOLE = (NZ * NY * 2 - 1) * REGION
WIDTH = 128
BF = jnp.bfloat16
F32 = jnp.float32
VMEM_LIMIT = 48 * 1024 * 1024


def groups_along(axes):
    ids = np.arange(NX * NZ * NY * NC).reshape(NX, NZ, NY, NC)
    size = int(np.prod([ids.shape[a] for a in axes]))
    return np.moveaxis(ids, axes, range(4 - len(axes), 4)).reshape(-1, size).tolist()


def exchange(value, axes):
    return lax.all_to_all(
        value, "d", split_axis=0, concat_axis=0, tiled=True, axis_index_groups=groups_along(axes)
    )


def of_both_cores(value):
    return lax.all_gather(value, "d", axis=0, axis_index_groups=groups_along((3,)))


def local_kernel(scale, core_ref, acts_hbm, cot_hbm, resid_hbm, count_hbm, rank_hbm,
                 resid_ref, keep_ref, give_ref,
                 acts_ref, cot_ref, acc_ref, count_ref, rank_ref, ranks_ref, chosen_ref, last_ref, pack_ref, sems):
    core = core_ref[0]
    steps, _, rows = acts_ref.shape
    cols = cot_ref.shape[2]
    tiles = cols // WIDTH
    groups = resid_ref.shape[1] // WIDTH

    copies = [
        pltpu.make_async_copy(rank_hbm, rank_ref, sems.at[0]),
        pltpu.make_async_copy(count_hbm, count_ref, sems.at[1]),
        pltpu.make_async_copy(resid_hbm, resid_ref, sems.at[2]),
    ]
    for s in range(steps):
        copies.append(pltpu.make_async_copy(acts_hbm.at[0, s], acts_ref.at[s], sems.at[3 + 2 * s]))
        copies.append(pltpu.make_async_copy(cot_hbm.at[0, s], cot_ref.at[s], sems.at[4 + 2 * s]))
    for i in [0, 1, 3, 4, 2] + list(range(5, 3 + 2 * steps)):
        copies[i].start()

    per = WIDTH // groups
    row_id = lax.broadcasted_iota(jnp.int32, (groups, WIDTH), 0)
    lane_id = lax.broadcasted_iota(jnp.int32, (groups, WIDTH), 1)
    owner_id = lax.broadcasted_iota(jnp.int32, (WIDTH, WIDTH), 0) % per
    block_id = lax.broadcasted_iota(jnp.int32, (WIDTH, WIDTH), 1) // REGION
    place = jnp.where(owner_id == block_id, 1.0, 0.0).astype(BF)
    eye = jnp.where(row_id == lane_id, 1.0, 0.0).astype(BF)
    copies[0].wait()
    copies[1].wait()
    for s in range(steps):
        for r in range(groups):
            ranks_ref[s, r:r + 1, :] = rank_ref[0, s:s + 1, r * WIDTH:(r + 1) * WIDTH]
        count = jnp.broadcast_to(count_ref[0, s:s + 1, :].astype(F32), (groups, WIDTH))
        spread = jnp.where(lane_id // per == row_id, count, 0.0)
        limit = jnp.dot(spread.astype(BF), place, preferred_element_type=F32)
        chosen = jnp.where(ranks_ref[s].astype(F32) < limit, 1.0, 0.0)
        if s == steps - 1:
            last_ref[...] = jnp.where(chosen > 0.5, ranks_ref[s].astype(F32), NONE)
        chosen_ref[s] = lax.dot_general(chosen.astype(BF), eye, (((0,), (0,)), ((), ())),
                                        preferred_element_type=F32)

    def multiply(s):
        copies[3 + 2 * s].wait()
        copies[4 + 2 * s].wait()
        left = acts_ref[s]
        half = 2 * WIDTH
        for h in range(cols // half):
            grad = lax.dot_general(left, cot_ref[s, :, h * half:(h + 1) * half],
                                   (((0,), (0,)), ((), ())), preferred_element_type=F32)
            grad = grad * scale
            for q in range(2):
                to = pl.ds(2 * h + q, rows, stride=tiles)
                acc_ref[s, to, :] = grad[:, q * WIDTH:(q + 1) * WIDTH]

    def select(s, me):
        columns = chosen_ref[s]
        for r in range(groups):
            span = slice(r * WIDTH, (r + 1) * WIDTH)
            total = resid_ref[0, span, :] + acc_ref[s, span, :]
            mask = jnp.broadcast_to(columns[:, r:r + 1], (WIDTH, WIDTH)) > 0.5
            resid_ref[0, span, :] = jnp.where(mask, 0.0, total)
            sent = jnp.where(mask, total, 0.0).astype(BF)
            for i in range(WIDTH // REGION):
                owner = r * (WIDTH // REGION) + i
                at = ((owner // NC) * steps + s) * REGION
                tile = sent[i * REGION:(i + 1) * REGION, :]
                if owner % NC == me:
                    keep_ref[at:at + REGION, :] = tile
                elif at < WHOLE:
                    give_ref[at:at + REGION, :] = tile
                else:
                    slots = last_ref[r:r + 1, :]
                    wide = jnp.broadcast_to(slots, (REGION, WIDTH))
                    slot = lax.broadcasted_iota(jnp.int32, (REGION, WIDTH), 0).astype(F32)
                    lane = lax.broadcasted_iota(jnp.int32, (REGION, WIDTH), 1)
                    pick = jnp.where((wide == slot) & (lane // REGION == i), 1.0, 0.0)
                    packed = jnp.dot(pick.astype(BF), sent, preferred_element_type=F32)
                    pack_ref[0:CAP, :] = packed[0:CAP, :]
                    pack_ref[CAP:2 * CAP, :] = jnp.broadcast_to(slots, (CAP, WIDTH))
                    give_ref[at:at + CAP + 2, :] = pack_ref[0:CAP + 2, :].astype(BF)

    multiply(0)
    copies[2].wait()
    for me in range(NC):
        @pl.when(core == me)
        def _(me=me):
            select(0, me)
            for s in range(1, steps):
                multiply(s)
                select(s, me)


def store_kernel(after_ref, value_ref, out_hbm, sem):
    copy = pltpu.make_async_copy(value_ref, out_hbm, sem)
    copy.start()
    copy.wait()


def pair_kernel(core_ref, keep_ref, both_ref, out_ref, tile_ref):
    core = core_ref[0]
    other = 1 - core
    chunk = 8 * REGION
    for at in range(0, WHOLE, chunk):
        span = slice(at, min(at + chunk, WHOLE))
        total = keep_ref[span, :].astype(F32) + both_ref[other, span, :].astype(F32)
        out_ref[span, :] = total.astype(BF)
    packed = both_ref[other, WHOLE:WHOLE + CAP, :].astype(F32)
    packed = jnp.concatenate([packed, jnp.zeros_like(packed)], axis=0).astype(BF)
    slots = both_ref[other, WHOLE + CAP:WHOLE + CAP + 2, :].astype(F32)[0:1, :]
    slot = lax.broadcasted_iota(jnp.int32, (REGION, WIDTH), 0).astype(F32)
    pick = jnp.where(jnp.broadcast_to(slots, (REGION, WIDTH)) == slot, 1.0, 0.0).astype(BF)
    tile_ref[...] = lax.dot_general(pick, packed, (((0,), (0,)), ((), ())), preferred_element_type=F32)
    at = pl.multiple_of(WIDTH - NC * REGION + core * REGION, REGION)
    total = keep_ref[WHOLE:WHOLE + REGION, :].astype(F32) + tile_ref[pl.ds(at, REGION), :]
    out_ref[WHOLE:WHOLE + REGION, :] = total.astype(BF)


def owner_kernel(arrived_ref, oresid_ref, count_ref, rank_ref, out_ref, last_ref, kept_ref):
    eye = (lax.broadcasted_iota(jnp.int32, (REGION, REGION), 0)
           == lax.broadcasted_iota(jnp.int32, (REGION, REGION), 1))
    oresid = oresid_ref[0]
    for s in range(rank_ref.shape[1]):
        total = arrived_ref[0, s].astype(F32)
        for k in range(1, arrived_ref.shape[0]):
            total = total + arrived_ref[k, s].astype(F32)
        count = jnp.broadcast_to(count_ref[0:1, s:s + 1], (1, REGION))
        row = jnp.where(rank_ref[0, s:s + 1, :] < count, 1.0, 0.0)
        square = jnp.where(eye, jnp.broadcast_to(row, (REGION, REGION)), 0.0)
        passed = jnp.broadcast_to(jnp.sum(square, axis=1, keepdims=True), (REGION, WIDTH)) > 0.5
        total = total + oresid
        going = jnp.where(passed, total, 0.0).astype(BF)
        oresid = jnp.where(passed, 0.0, total)
        for k in range(out_ref.shape[0]):
            out_ref[k, s] = going
    last_ref[...] = total
    kept_ref[...] = jnp.where(passed, 0.0, 1.0)


def update_kernel(arrived_ref, out_ref):
    total = jnp.zeros((REGION, WIDTH), F32)
    for s in range(arrived_ref.shape[1]):
        cross = arrived_ref[0, s].astype(F32)
        for x in range(1, NX):
            cross = cross + arrived_ref[x, s].astype(F32)
        total = total + cross.astype(BF).astype(F32)
    applied = (-STEP_SIZE * total).astype(BF)
    for k in range(out_ref.shape[0]):
        out_ref[k] = applied


def assemble_kernel(halves_ref, last_ref, kept_ref, out_ref, oresid_ref, flat_ref):
    oresid_ref[0] = jnp.where(kept_ref[...] > 0.5, last_ref[...], 0.0)
    rows, cols = out_ref.shape
    tiles = cols // WIDTH
    for i in range(CHIPS):
        for c in range(NC):
            at = (i * NC + c) * REGION
            flat_ref[at:at + REGION, :] = halves_ref[c, i].astype(F32)
    for t in range(tiles):
        out_ref[:, t * WIDTH:(t + 1) * WIDTH] = flat_ref[pl.ds(t, rows, stride=tiles), :].astype(BF)


def vmem():
    return pl.BlockSpec(memory_space=pltpu.VMEM)


def hbm():
    return pl.BlockSpec(memory_space=pltpu.HBM)


def smem():
    return pl.BlockSpec(memory_space=pltpu.SMEM)


def per_device(acts, cotangent, residual, owner_residual, in_count, in_rank, out_count, out_rank):
    steps, tokens, rows = acts.shape[1:]
    cols = cotangent.shape[3]
    blocks = residual.shape[1]
    scale = 1.0 / math.sqrt(tokens * CHIPS * NC)
    core = (lax.axis_index("d") % NC).astype(jnp.int32).reshape(1)
    params = pltpu.CompilerParams(vmem_limit_bytes=VMEM_LIMIT)

    def local(*args):
        return local_kernel(scale, *args)

    size = CHIPS * steps * REGION
    new_resid, keep, give = pl.pallas_call(
        local,
        in_specs=[smem(), hbm(), hbm(), hbm(), hbm(), hbm()],
        out_specs=[vmem(), vmem(), vmem()],
        out_shape=[
            pltpu.VMEM(residual.shape, F32),
            jax.ShapeDtypeStruct((size, WIDTH), BF),
            jax.ShapeDtypeStruct((WHOLE + CAP + 2, WIDTH), BF),
        ],
        scratch_shapes=[
            pltpu.VMEM((steps, tokens, rows), BF),
            pltpu.VMEM((steps, tokens, cols), BF),
            pltpu.VMEM((steps, blocks, WIDTH), F32),
            pltpu.VMEM(in_count.shape, jnp.int32),
            pltpu.VMEM(in_rank.shape, jnp.int32),
            pltpu.VMEM((steps, blocks // WIDTH, WIDTH), jnp.int32),
            pltpu.VMEM((steps, WIDTH, WIDTH), F32),
            pltpu.VMEM((blocks // WIDTH, WIDTH), F32),
            pltpu.VMEM((2 * CAP, WIDTH), F32),
            pltpu.SemaphoreType.DMA((3 + 2 * steps,)),
        ],
        compiler_params=params,
        name="local",
    )(core, *[pltpu.with_memory_space_constraint(v, pltpu.HBM)
            for v in (acts, cotangent, residual, in_count, in_rank)])

    pair = pl.pallas_call(
        pair_kernel,
        in_specs=[smem(), vmem(), vmem()],
        out_specs=vmem(),
        out_shape=jax.ShapeDtypeStruct((size, WIDTH), BF),
        scratch_shapes=[pltpu.VMEM((WIDTH, WIDTH), F32)],
        compiler_params=params,
        name="pair",
    )(core, keep, of_both_cores(give))
    pair = pair.reshape(CHIPS, steps, REGION, WIDTH)
    arrived = exchange(pair, (1, 2))

    tile = jax.ShapeDtypeStruct((REGION, WIDTH), F32)
    outgoing, last, kept = pl.pallas_call(
        owner_kernel,
        in_specs=[vmem(), vmem(), vmem(), vmem()],
        out_specs=[vmem(), vmem(), vmem()],
        out_shape=[jax.ShapeDtypeStruct((NX, steps, REGION, WIDTH), BF), tile, tile],
        compiler_params=params,
        name="owner",
    )(arrived, owner_residual, out_count, out_rank)

    new_residual = pl.pallas_call(
        store_kernel,
        in_specs=[pl.BlockSpec(memory_space=pl.ANY), vmem()],
        out_specs=hbm(),
        out_shape=jax.ShapeDtypeStruct(residual.shape, F32),
        scratch_shapes=[pltpu.SemaphoreType.DMA],
        compiler_params=params,
        name="store",
    )(last, new_resid)
    copies = pl.pallas_call(
        update_kernel,
        in_specs=[vmem()],
        out_specs=vmem(),
        out_shape=jax.ShapeDtypeStruct((CHIPS, REGION, WIDTH), BF),
        compiler_params=params,
        name="update",
    )(exchange(outgoing, (0,)))
    copies, new_residual = lax.optimization_barrier((copies, new_residual))
    halves = of_both_cores(exchange(copies, (1, 2)))
    applied, new_owner = pl.pallas_call(
        assemble_kernel,
        in_specs=[vmem(), vmem(), vmem()],
        out_specs=[vmem(), vmem()],
        out_shape=[
            jax.ShapeDtypeStruct((rows, cols), BF),
            jax.ShapeDtypeStruct(owner_residual.shape, F32),
        ],
        scratch_shapes=[
            pltpu.VMEM((blocks, WIDTH), F32),
        ],
        compiler_params=params,
        name="assemble",
    )(halves, last, kept)
    return applied, new_residual, new_owner


def solution(mesh):
    flat = Mesh(mesh.devices.reshape(-1), ("d",))
    spec = P("d")
    return jax.shard_map(
        per_device,
        mesh=flat,
        in_specs=(spec,) * 8,
        out_specs=(P(), spec, spec),
        check_vma=False,
    )
```

```python
import math

import jax
import jax.numpy as jnp
import numpy as np
from jax import lax
from jax.experimental import pallas as pl
from jax.experimental.pallas import tpu as pltpu
from jax.sharding import Mesh
from jax.sharding import PartitionSpec as P

STEP_SIZE = 0.0625
NX, NZ, NY, NC = 4, 8, 8, 2
CHIPS = NZ * NY
REGION = 16
CAP = 8
NONE = 31.0
WHOLE = (NZ * NY * 2 - 1) * REGION
WIDTH = 128
BF = jnp.bfloat16
F32 = jnp.float32
VMEM_LIMIT = 48 * 1024 * 1024


def groups_along(axes):
    ids = np.arange(NX * NZ * NY * NC).reshape(NX, NZ, NY, NC)
    size = int(np.prod([ids.shape[a] for a in axes]))
    return np.moveaxis(ids, axes, range(4 - len(axes), 4)).reshape(-1, size).tolist()


def place_of(core, z, y):
    return z * NY + y if core == 0 else y * NZ + z


def chips_in_place():
    ids = np.arange(NX * NZ * NY * NC).reshape(NX, NZ, NY, NC)
    first, second = ids[..., 0], ids[..., 1].swapaxes(1, 2)
    return first.reshape(NX, -1).tolist() + second.reshape(NX, -1).tolist()


def exchange(value, groups):
    return lax.all_to_all(
        value, "d", split_axis=0, concat_axis=0, tiled=True, axis_index_groups=groups
    )


def of_both_cores(value):
    return lax.all_gather(value, "d", axis=0, axis_index_groups=groups_along((3,)))


def local_kernel(scale, core_ref, acts_hbm, cot_hbm, resid_hbm, count_hbm, rank_hbm,
                 resid_ref, keep_ref, give_ref,
                 acts_ref, cot_ref, acc_ref, count_ref, rank_ref, ranks_ref, chosen_ref, last_ref, pack_ref, sems):
    core = core_ref[0]
    steps, _, rows = acts_ref.shape
    cols = cot_ref.shape[2]
    tiles = cols // WIDTH
    groups = resid_ref.shape[1] // WIDTH

    copies = [
        pltpu.make_async_copy(rank_hbm, rank_ref, sems.at[0]),
        pltpu.make_async_copy(count_hbm, count_ref, sems.at[1]),
        pltpu.make_async_copy(resid_hbm, resid_ref, sems.at[2]),
    ]
    for s in range(steps):
        copies.append(pltpu.make_async_copy(acts_hbm.at[0, s], acts_ref.at[s], sems.at[3 + 2 * s]))
        copies.append(pltpu.make_async_copy(cot_hbm.at[0, s], cot_ref.at[s], sems.at[4 + 2 * s]))
    for i in [0, 1, 3, 4, 2] + list(range(5, 3 + 2 * steps)):
        copies[i].start()

    per = WIDTH // groups
    row_id = lax.broadcasted_iota(jnp.int32, (groups, WIDTH), 0)
    lane_id = lax.broadcasted_iota(jnp.int32, (groups, WIDTH), 1)
    owner_id = lax.broadcasted_iota(jnp.int32, (WIDTH, WIDTH), 0) % per
    block_id = lax.broadcasted_iota(jnp.int32, (WIDTH, WIDTH), 1) // REGION
    place = jnp.where(owner_id == block_id, 1.0, 0.0).astype(BF)
    eye = jnp.where(row_id == lane_id, 1.0, 0.0).astype(BF)
    copies[0].wait()
    copies[1].wait()
    for s in range(steps):
        for r in range(groups):
            ranks_ref[s, r:r + 1, :] = rank_ref[0, s:s + 1, r * WIDTH:(r + 1) * WIDTH]
        count = jnp.broadcast_to(count_ref[0, s:s + 1, :].astype(F32), (groups, WIDTH))
        spread = jnp.where(lane_id // per == row_id, count, 0.0)
        limit = jnp.dot(spread.astype(BF), place, preferred_element_type=F32)
        chosen = jnp.where(ranks_ref[s].astype(F32) < limit, 1.0, 0.0)
        if s == steps - 1:
            last_ref[...] = jnp.where(chosen > 0.5, ranks_ref[s].astype(F32), NONE)
        chosen_ref[s] = lax.dot_general(chosen.astype(BF), eye, (((0,), (0,)), ((), ())),
                                        preferred_element_type=F32)

    def multiply(s):
        copies[3 + 2 * s].wait()
        copies[4 + 2 * s].wait()
        left = acts_ref[s]
        half = 2 * WIDTH
        for h in range(cols // half):
            grad = lax.dot_general(left, cot_ref[s, :, h * half:(h + 1) * half],
                                   (((0,), (0,)), ((), ())), preferred_element_type=F32)
            grad = grad * scale
            for q in range(2):
                to = pl.ds(2 * h + q, rows, stride=tiles)
                acc_ref[s, to, :] = grad[:, q * WIDTH:(q + 1) * WIDTH]

    def select(s, me):
        columns = chosen_ref[s]
        for r in range(groups):
            span = slice(r * WIDTH, (r + 1) * WIDTH)
            total = resid_ref[0, span, :] + acc_ref[s, span, :]
            mask = jnp.broadcast_to(columns[:, r:r + 1], (WIDTH, WIDTH)) > 0.5
            resid_ref[0, span, :] = jnp.where(mask, 0.0, total)
            sent = jnp.where(mask, total, 0.0).astype(BF)
            for i in range(WIDTH // REGION):
                owner = r * (WIDTH // REGION) + i
                z, y, c = owner // (NY * NC), (owner // NC) % NY, owner % NC
                at = (place_of(c, z, y) * steps + s) * REGION
                tile = sent[i * REGION:(i + 1) * REGION, :]
                if owner % NC == me:
                    keep_ref[at:at + REGION, :] = tile
                elif at < WHOLE:
                    give_ref[at:at + REGION, :] = tile
                else:
                    slots = last_ref[r:r + 1, :]
                    wide = jnp.broadcast_to(slots, (REGION, WIDTH))
                    slot = lax.broadcasted_iota(jnp.int32, (REGION, WIDTH), 0).astype(F32)
                    lane = lax.broadcasted_iota(jnp.int32, (REGION, WIDTH), 1)
                    pick = jnp.where((wide == slot) & (lane // REGION == i), 1.0, 0.0)
                    packed = jnp.dot(pick.astype(BF), sent, preferred_element_type=F32)
                    pack_ref[0:CAP, :] = packed[0:CAP, :]
                    pack_ref[CAP:2 * CAP, :] = jnp.broadcast_to(slots, (CAP, WIDTH))
                    give_ref[at:at + CAP + 2, :] = pack_ref[0:CAP + 2, :].astype(BF)

    multiply(0)
    copies[2].wait()
    for me in range(NC):
        @pl.when(core == me)
        def _(me=me):
            select(0, me)
            for s in range(1, steps):
                multiply(s)
                select(s, me)


def store_kernel(after_ref, value_ref, out_hbm, sem):
    copy = pltpu.make_async_copy(value_ref, out_hbm, sem)
    copy.start()
    copy.wait()


def pair_kernel(core_ref, keep_ref, both_ref, out_ref, tile_ref):
    core = core_ref[0]
    other = 1 - core
    chunk = 8 * REGION
    for at in range(0, WHOLE, chunk):
        span = slice(at, min(at + chunk, WHOLE))
        total = keep_ref[span, :].astype(F32) + both_ref[other, span, :].astype(F32)
        out_ref[span, :] = total.astype(BF)
    packed = both_ref[other, WHOLE:WHOLE + CAP, :].astype(F32)
    packed = jnp.concatenate([packed, jnp.zeros_like(packed)], axis=0).astype(BF)
    slots = both_ref[other, WHOLE + CAP:WHOLE + CAP + 2, :].astype(F32)[0:1, :]
    slot = lax.broadcasted_iota(jnp.int32, (REGION, WIDTH), 0).astype(F32)
    pick = jnp.where(jnp.broadcast_to(slots, (REGION, WIDTH)) == slot, 1.0, 0.0).astype(BF)
    tile_ref[...] = lax.dot_general(pick, packed, (((0,), (0,)), ((), ())), preferred_element_type=F32)
    at = pl.multiple_of(WIDTH - NC * REGION + core * REGION, REGION)
    total = keep_ref[WHOLE:WHOLE + REGION, :].astype(F32) + tile_ref[pl.ds(at, REGION), :]
    out_ref[WHOLE:WHOLE + REGION, :] = total.astype(BF)


def owner_kernel(arrived_ref, oresid_ref, count_ref, rank_ref, out_ref, last_ref, kept_ref):
    eye = (lax.broadcasted_iota(jnp.int32, (REGION, REGION), 0)
           == lax.broadcasted_iota(jnp.int32, (REGION, REGION), 1))
    oresid = oresid_ref[0]
    for s in range(rank_ref.shape[1]):
        total = arrived_ref[0, s].astype(F32)
        for k in range(1, arrived_ref.shape[0]):
            total = total + arrived_ref[k, s].astype(F32)
        count = jnp.broadcast_to(count_ref[0:1, s:s + 1], (1, REGION))
        row = jnp.where(rank_ref[0, s:s + 1, :] < count, 1.0, 0.0)
        square = jnp.where(eye, jnp.broadcast_to(row, (REGION, REGION)), 0.0)
        passed = jnp.broadcast_to(jnp.sum(square, axis=1, keepdims=True), (REGION, WIDTH)) > 0.5
        total = total + oresid
        going = jnp.where(passed, total, 0.0).astype(BF)
        oresid = jnp.where(passed, 0.0, total)
        for k in range(out_ref.shape[0]):
            out_ref[k, s] = going
    last_ref[...] = total
    kept_ref[...] = jnp.where(passed, 0.0, 1.0)


def update_kernel(arrived_ref, out_ref):
    total = jnp.zeros((REGION, WIDTH), F32)
    for s in range(arrived_ref.shape[1]):
        cross = arrived_ref[0, s].astype(F32)
        for x in range(1, NX):
            cross = cross + arrived_ref[x, s].astype(F32)
        total = total + cross.astype(BF).astype(F32)
    applied = (-STEP_SIZE * total).astype(BF)
    for k in range(out_ref.shape[0]):
        out_ref[k] = applied


def assemble_kernel(halves_ref, last_ref, kept_ref, out_ref, oresid_ref, flat_ref):
    oresid_ref[0] = jnp.where(kept_ref[...] > 0.5, last_ref[...], 0.0)
    rows, cols = out_ref.shape
    tiles = cols // WIDTH
    for i in range(CHIPS):
        for c in range(NC):
            at = (i * NC + c) * REGION
            flat_ref[at:at + REGION, :] = halves_ref[c, i].astype(F32)
    for t in range(tiles):
        out_ref[:, t * WIDTH:(t + 1) * WIDTH] = flat_ref[pl.ds(t, rows, stride=tiles), :].astype(BF)


def vmem():
    return pl.BlockSpec(memory_space=pltpu.VMEM)


def hbm():
    return pl.BlockSpec(memory_space=pltpu.HBM)


def smem():
    return pl.BlockSpec(memory_space=pltpu.SMEM)


def per_device(acts, cotangent, residual, owner_residual, in_count, in_rank, out_count, out_rank):
    steps, tokens, rows = acts.shape[1:]
    cols = cotangent.shape[3]
    blocks = residual.shape[1]
    scale = 1.0 / math.sqrt(tokens * CHIPS * NC)
    core = (lax.axis_index("d") % NC).astype(jnp.int32).reshape(1)
    params = pltpu.CompilerParams(vmem_limit_bytes=VMEM_LIMIT)

    def local(*args):
        return local_kernel(scale, *args)

    size = CHIPS * steps * REGION
    new_resid, keep, give = pl.pallas_call(
        local,
        in_specs=[smem(), hbm(), hbm(), hbm(), hbm(), hbm()],
        out_specs=[vmem(), vmem(), vmem()],
        out_shape=[
            pltpu.VMEM(residual.shape, F32),
            jax.ShapeDtypeStruct((size, WIDTH), BF),
            jax.ShapeDtypeStruct((WHOLE + CAP + 2, WIDTH), BF),
        ],
        scratch_shapes=[
            pltpu.VMEM((steps, tokens, rows), BF),
            pltpu.VMEM((steps, tokens, cols), BF),
            pltpu.VMEM((steps, blocks, WIDTH), F32),
            pltpu.VMEM(in_count.shape, jnp.int32),
            pltpu.VMEM(in_rank.shape, jnp.int32),
            pltpu.VMEM((steps, blocks // WIDTH, WIDTH), jnp.int32),
            pltpu.VMEM((steps, WIDTH, WIDTH), F32),
            pltpu.VMEM((blocks // WIDTH, WIDTH), F32),
            pltpu.VMEM((2 * CAP, WIDTH), F32),
            pltpu.SemaphoreType.DMA((3 + 2 * steps,)),
        ],
        compiler_params=params,
        name="local",
    )(core, *[pltpu.with_memory_space_constraint(v, pltpu.HBM)
            for v in (acts, cotangent, residual, in_count, in_rank)])

    pair = pl.pallas_call(
        pair_kernel,
        in_specs=[smem(), vmem(), vmem()],
        out_specs=vmem(),
        out_shape=jax.ShapeDtypeStruct((size, WIDTH), BF),
        scratch_shapes=[pltpu.VMEM((WIDTH, WIDTH), F32)],
        compiler_params=params,
        name="pair",
    )(core, keep, of_both_cores(give))
    pair = pair.reshape(CHIPS, steps, REGION, WIDTH)
    arrived = exchange(pair, chips_in_place())

    tile = jax.ShapeDtypeStruct((REGION, WIDTH), F32)
    outgoing, last, kept = pl.pallas_call(
        owner_kernel,
        in_specs=[vmem(), vmem(), vmem(), vmem()],
        out_specs=[vmem(), vmem(), vmem()],
        out_shape=[jax.ShapeDtypeStruct((NX, steps, REGION, WIDTH), BF), tile, tile],
        compiler_params=params,
        name="owner",
    )(arrived, owner_residual, out_count, out_rank)

    new_residual = pl.pallas_call(
        store_kernel,
        in_specs=[pl.BlockSpec(memory_space=pl.ANY), vmem()],
        out_specs=hbm(),
        out_shape=jax.ShapeDtypeStruct(residual.shape, F32),
        scratch_shapes=[pltpu.SemaphoreType.DMA],
        compiler_params=params,
        name="store",
    )(last, new_resid)
    copies = pl.pallas_call(
        update_kernel,
        in_specs=[vmem()],
        out_specs=vmem(),
        out_shape=jax.ShapeDtypeStruct((CHIPS, REGION, WIDTH), BF),
        compiler_params=params,
        name="update",
    )(exchange(outgoing, groups_along((0,))))
    copies, new_residual = lax.optimization_barrier((copies, new_residual))
    halves = of_both_cores(exchange(copies, groups_along((1, 2))))
    applied, new_owner = pl.pallas_call(
        assemble_kernel,
        in_specs=[vmem(), vmem(), vmem()],
        out_specs=[vmem(), vmem()],
        out_shape=[
            jax.ShapeDtypeStruct((rows, cols), BF),
            jax.ShapeDtypeStruct(owner_residual.shape, F32),
        ],
        scratch_shapes=[
            pltpu.VMEM((blocks, WIDTH), F32),
        ],
        compiler_params=params,
        name="assemble",
    )(halves, last, kept)
    return applied, new_residual, new_owner


def solution(mesh):
    flat = Mesh(mesh.devices.reshape(-1), ("d",))
    spec = P("d")
    return jax.shard_map(
        per_device,
        mesh=flat,
        in_specs=(spec,) * 8,
        out_specs=(P(), spec, spec),
        check_vma=False,
    )
```

```python
import math

import jax
import jax.numpy as jnp
import numpy as np
from jax import lax
from jax.experimental import pallas as pl
from jax.experimental.pallas import tpu as pltpu
from jax.sharding import Mesh
from jax.sharding import PartitionSpec as P

STEP_SIZE = 0.0625
NX, NZ, NY, NC = 4, 8, 8, 2
CHIPS = NZ * NY
REGION = 16
CAP = 8
NONE = 31.0
WHOLE = (NZ * NY * 2 - 1) * REGION
WIDTH = 128
BF = jnp.bfloat16
F32 = jnp.float32
VMEM_LIMIT = 48 * 1024 * 1024


def groups_along(axes):
    ids = np.arange(NX * NZ * NY * NC).reshape(NX, NZ, NY, NC)
    size = int(np.prod([ids.shape[a] for a in axes]))
    return np.moveaxis(ids, axes, range(4 - len(axes), 4)).reshape(-1, size).tolist()


def exchange(value, axes):
    return lax.all_to_all(
        value, "d", split_axis=0, concat_axis=0, tiled=True, axis_index_groups=groups_along(axes)
    )


def of_both_cores(value):
    return lax.all_gather(value, "d", axis=0, axis_index_groups=groups_along((3,)))


def local_kernel(scale, core_ref, acts_hbm, cot_hbm, resid_hbm, count_hbm, rank_hbm,
                 resid_ref, keep_ref, give_ref,
                 acts_ref, cot_ref, acc_ref, count_ref, rank_ref, ranks_ref, chosen_ref, last_ref, pack_ref, sems):
    core = core_ref[0]
    steps, _, rows = acts_ref.shape
    cols = cot_ref.shape[2]
    tiles = cols // WIDTH
    groups = resid_ref.shape[1] // WIDTH

    copies = [
        pltpu.make_async_copy(rank_hbm, rank_ref, sems.at[0]),
        pltpu.make_async_copy(count_hbm, count_ref, sems.at[1]),
        pltpu.make_async_copy(resid_hbm, resid_ref, sems.at[2]),
    ]
    for s in range(steps):
        copies.append(pltpu.make_async_copy(acts_hbm.at[0, s], acts_ref.at[s], sems.at[3 + 2 * s]))
        copies.append(pltpu.make_async_copy(cot_hbm.at[0, s], cot_ref.at[s], sems.at[4 + 2 * s]))
    for i in [0, 1, 3, 4, 2] + list(range(5, 3 + 2 * steps)):
        copies[i].start()

    per = WIDTH // groups
    row_id = lax.broadcasted_iota(jnp.int32, (groups, WIDTH), 0)
    lane_id = lax.broadcasted_iota(jnp.int32, (groups, WIDTH), 1)
    owner_id = lax.broadcasted_iota(jnp.int32, (WIDTH, WIDTH), 0) % per
    block_id = lax.broadcasted_iota(jnp.int32, (WIDTH, WIDTH), 1) // REGION
    place = jnp.where(owner_id == block_id, 1.0, 0.0).astype(BF)
    eye = jnp.where(row_id == lane_id, 1.0, 0.0).astype(BF)
    copies[0].wait()
    copies[1].wait()
    for s in range(steps):
        for r in range(groups):
            ranks_ref[s, r:r + 1, :] = rank_ref[0, s:s + 1, r * WIDTH:(r + 1) * WIDTH]
        count = jnp.broadcast_to(count_ref[0, s:s + 1, :].astype(F32), (groups, WIDTH))
        spread = jnp.where(lane_id // per == row_id, count, 0.0)
        limit = jnp.dot(spread.astype(BF), place, preferred_element_type=F32)
        chosen = jnp.where(ranks_ref[s].astype(F32) < limit, 1.0, 0.0)
        if s == steps - 1:
            last_ref[...] = jnp.where(chosen > 0.5, ranks_ref[s].astype(F32), NONE)
        chosen_ref[s] = lax.dot_general(chosen.astype(BF), eye, (((0,), (0,)), ((), ())),
                                        preferred_element_type=F32)

    def multiply(s):
        copies[3 + 2 * s].wait()
        copies[4 + 2 * s].wait()
        left = acts_ref[s]
        half = 2 * WIDTH
        for h in range(cols // half):
            grad = lax.dot_general(left, cot_ref[s, :, h * half:(h + 1) * half],
                                   (((0,), (0,)), ((), ())), preferred_element_type=F32)
            grad = grad * scale
            for q in range(2):
                to = pl.ds(2 * h + q, rows, stride=tiles)
                acc_ref[s, to, :] = grad[:, q * WIDTH:(q + 1) * WIDTH]

    def select(s, me):
        columns = chosen_ref[s]
        for r in range(groups):
            span = slice(r * WIDTH, (r + 1) * WIDTH)
            total = resid_ref[0, span, :] + acc_ref[s, span, :]
            mask = jnp.broadcast_to(columns[:, r:r + 1], (WIDTH, WIDTH)) > 0.5
            resid_ref[0, span, :] = jnp.where(mask, 0.0, total)
            sent = jnp.where(mask, total, 0.0).astype(BF)
            for i in range(WIDTH // REGION):
                owner = r * (WIDTH // REGION) + i
                at = ((owner // NC) * steps + s) * REGION
                tile = sent[i * REGION:(i + 1) * REGION, :]
                if owner % NC == me:
                    keep_ref[at:at + REGION, :] = tile
                elif at < WHOLE:
                    give_ref[at:at + REGION, :] = tile
                else:
                    slots = last_ref[r:r + 1, :]
                    wide = jnp.broadcast_to(slots, (REGION, WIDTH))
                    slot = lax.broadcasted_iota(jnp.int32, (REGION, WIDTH), 0).astype(F32)
                    lane = lax.broadcasted_iota(jnp.int32, (REGION, WIDTH), 1)
                    pick = jnp.where((wide == slot) & (lane // REGION == i), 1.0, 0.0)
                    packed = jnp.dot(pick.astype(BF), sent, preferred_element_type=F32)
                    pack_ref[0:CAP, :] = packed[0:CAP, :]
                    pack_ref[CAP:2 * CAP, :] = jnp.broadcast_to(slots, (CAP, WIDTH))
                    give_ref[at:at + CAP + 2, :] = pack_ref[0:CAP + 2, :].astype(BF)

    multiply(0)
    copies[2].wait()
    for me in range(NC):
        @pl.when(core == me)
        def _(me=me):
            select(0, me)
            for s in range(1, steps):
                multiply(s)
                select(s, me)


def stored_by(me, core_ref, resid_ref, store_hbm, sem):
    @pl.when(core_ref[0] == me)
    def _():
        copy = pltpu.make_async_copy(resid_ref, store_hbm, sem)
        copy.start()
        copy.wait()


def late_kernel(core_ref, after_ref, resid_ref, begun_hbm, store_hbm, sem):
    stored_by(1, core_ref, resid_ref, store_hbm, sem)


def pair_kernel(core_ref, keep_ref, both_ref, resid_ref, out_ref, store_hbm, tile_ref, sem):
    core = core_ref[0]
    other = 1 - core
    chunk = 8 * REGION
    for at in range(0, WHOLE, chunk):
        span = slice(at, min(at + chunk, WHOLE))
        total = keep_ref[span, :].astype(F32) + both_ref[other, span, :].astype(F32)
        out_ref[span, :] = total.astype(BF)
    packed = both_ref[other, WHOLE:WHOLE + CAP, :].astype(F32)
    packed = jnp.concatenate([packed, jnp.zeros_like(packed)], axis=0).astype(BF)
    slots = both_ref[other, WHOLE + CAP:WHOLE + CAP + 2, :].astype(F32)[0:1, :]
    slot = lax.broadcasted_iota(jnp.int32, (REGION, WIDTH), 0).astype(F32)
    pick = jnp.where(jnp.broadcast_to(slots, (REGION, WIDTH)) == slot, 1.0, 0.0).astype(BF)
    tile_ref[...] = lax.dot_general(pick, packed, (((0,), (0,)), ((), ())), preferred_element_type=F32)
    at = pl.multiple_of(WIDTH - NC * REGION + core * REGION, REGION)
    total = keep_ref[WHOLE:WHOLE + REGION, :].astype(F32) + tile_ref[pl.ds(at, REGION), :]
    out_ref[WHOLE:WHOLE + REGION, :] = total.astype(BF)
    stored_by(0, core_ref, resid_ref, store_hbm, sem)


def owner_kernel(arrived_ref, oresid_ref, count_ref, rank_ref, out_ref, last_ref, kept_ref):
    eye = (lax.broadcasted_iota(jnp.int32, (REGION, REGION), 0)
           == lax.broadcasted_iota(jnp.int32, (REGION, REGION), 1))
    oresid = oresid_ref[0]
    for s in range(rank_ref.shape[1]):
        total = arrived_ref[0, s].astype(F32)
        for k in range(1, arrived_ref.shape[0]):
            total = total + arrived_ref[k, s].astype(F32)
        count = jnp.broadcast_to(count_ref[0:1, s:s + 1], (1, REGION))
        row = jnp.where(rank_ref[0, s:s + 1, :] < count, 1.0, 0.0)
        square = jnp.where(eye, jnp.broadcast_to(row, (REGION, REGION)), 0.0)
        passed = jnp.broadcast_to(jnp.sum(square, axis=1, keepdims=True), (REGION, WIDTH)) > 0.5
        total = total + oresid
        going = jnp.where(passed, total, 0.0).astype(BF)
        oresid = jnp.where(passed, 0.0, total)
        for k in range(out_ref.shape[0]):
            out_ref[k, s] = going
    last_ref[...] = total
    kept_ref[...] = jnp.where(passed, 0.0, 1.0)


def update_kernel(arrived_ref, out_ref):
    total = jnp.zeros((REGION, WIDTH), F32)
    for s in range(arrived_ref.shape[1]):
        cross = arrived_ref[0, s].astype(F32)
        for x in range(1, NX):
            cross = cross + arrived_ref[x, s].astype(F32)
        total = total + cross.astype(BF).astype(F32)
    applied = (-STEP_SIZE * total).astype(BF)
    for k in range(out_ref.shape[0]):
        out_ref[k] = applied


def assemble_kernel(halves_ref, last_ref, kept_ref, out_ref, oresid_ref, flat_ref):
    oresid_ref[0] = jnp.where(kept_ref[...] > 0.5, last_ref[...], 0.0)
    rows, cols = out_ref.shape
    tiles = cols // WIDTH
    for i in range(CHIPS):
        for c in range(NC):
            at = (i * NC + c) * REGION
            flat_ref[at:at + REGION, :] = halves_ref[c, i].astype(F32)
    for t in range(tiles):
        out_ref[:, t * WIDTH:(t + 1) * WIDTH] = flat_ref[pl.ds(t, rows, stride=tiles), :].astype(BF)


def vmem():
    return pl.BlockSpec(memory_space=pltpu.VMEM)


def hbm():
    return pl.BlockSpec(memory_space=pltpu.HBM)


def smem():
    return pl.BlockSpec(memory_space=pltpu.SMEM)


def per_device(acts, cotangent, residual, owner_residual, in_count, in_rank, out_count, out_rank):
    steps, tokens, rows = acts.shape[1:]
    cols = cotangent.shape[3]
    blocks = residual.shape[1]
    scale = 1.0 / math.sqrt(tokens * CHIPS * NC)
    core = (lax.axis_index("d") % NC).astype(jnp.int32).reshape(1)
    params = pltpu.CompilerParams(vmem_limit_bytes=VMEM_LIMIT)

    def local(*args):
        return local_kernel(scale, *args)

    size = CHIPS * steps * REGION
    new_resid, keep, give = pl.pallas_call(
        local,
        in_specs=[smem(), hbm(), hbm(), hbm(), hbm(), hbm()],
        out_specs=[vmem(), vmem(), vmem()],
        out_shape=[
            pltpu.VMEM(residual.shape, F32),
            jax.ShapeDtypeStruct((size, WIDTH), BF),
            jax.ShapeDtypeStruct((WHOLE + CAP + 2, WIDTH), BF),
        ],
        scratch_shapes=[
            pltpu.VMEM((steps, tokens, rows), BF),
            pltpu.VMEM((steps, tokens, cols), BF),
            pltpu.VMEM((steps, blocks, WIDTH), F32),
            pltpu.VMEM(in_count.shape, jnp.int32),
            pltpu.VMEM(in_rank.shape, jnp.int32),
            pltpu.VMEM((steps, blocks // WIDTH, WIDTH), jnp.int32),
            pltpu.VMEM((steps, WIDTH, WIDTH), F32),
            pltpu.VMEM((blocks // WIDTH, WIDTH), F32),
            pltpu.VMEM((2 * CAP, WIDTH), F32),
            pltpu.SemaphoreType.DMA((3 + 2 * steps,)),
        ],
        compiler_params=params,
        name="local",
    )(core, *[pltpu.with_memory_space_constraint(v, pltpu.HBM)
            for v in (acts, cotangent, residual, in_count, in_rank)])

    placed = jax.ShapeDtypeStruct(residual.shape, F32)
    pair, store = pl.pallas_call(
        pair_kernel,
        in_specs=[smem(), vmem(), vmem(), vmem()],
        out_specs=[vmem(), hbm()],
        out_shape=[jax.ShapeDtypeStruct((size, WIDTH), BF), placed],
        scratch_shapes=[pltpu.VMEM((WIDTH, WIDTH), F32), pltpu.SemaphoreType.DMA],
        compiler_params=params,
        name="pair",
    )(core, keep, of_both_cores(give), new_resid)
    pair = pair.reshape(CHIPS, steps, REGION, WIDTH)
    arrived = exchange(pair, (1, 2))

    tile = jax.ShapeDtypeStruct((REGION, WIDTH), F32)
    outgoing, last, kept = pl.pallas_call(
        owner_kernel,
        in_specs=[vmem(), vmem(), vmem(), vmem()],
        out_specs=[vmem(), vmem(), vmem()],
        out_shape=[jax.ShapeDtypeStruct((NX, steps, REGION, WIDTH), BF), tile, tile],
        compiler_params=params,
        name="owner",
    )(arrived, owner_residual, out_count, out_rank)

    copies = pl.pallas_call(
        update_kernel,
        in_specs=[vmem()],
        out_specs=vmem(),
        out_shape=jax.ShapeDtypeStruct((CHIPS, REGION, WIDTH), BF),
        compiler_params=params,
        name="update",
    )(exchange(outgoing, (0,)))
    own = exchange(copies, (1, 2))
    new_residual = pl.pallas_call(
        late_kernel,
        in_specs=[smem(), pl.BlockSpec(memory_space=pl.ANY), vmem(), hbm()],
        out_specs=hbm(),
        out_shape=placed,
        scratch_shapes=[pltpu.SemaphoreType.DMA],
        input_output_aliases={3: 0},
        compiler_params=params,
        name="late",
    )(core, own, new_resid, store)
    own, new_residual = lax.optimization_barrier((own, new_residual))
    halves = of_both_cores(own)
    applied, new_owner = pl.pallas_call(
        assemble_kernel,
        in_specs=[vmem(), vmem(), vmem()],
        out_specs=[vmem(), vmem()],
        out_shape=[
            jax.ShapeDtypeStruct((rows, cols), BF),
            jax.ShapeDtypeStruct(owner_residual.shape, F32),
        ],
        scratch_shapes=[
            pltpu.VMEM((blocks, WIDTH), F32),
        ],
        compiler_params=params,
        name="assemble",
    )(halves, last, kept)
    return applied, new_residual, new_owner


def solution(mesh):
    flat = Mesh(mesh.devices.reshape(-1), ("d",))
    spec = P("d")
    return jax.shard_map(
        per_device,
        mesh=flat,
        in_specs=(spec,) * 8,
        out_specs=(P(), spec, spec),
        check_vma=False,
    )
```

```python
import math

import jax
import jax.numpy as jnp
import numpy as np
from jax import lax
from jax.experimental import pallas as pl
from jax.experimental.pallas import tpu as pltpu
from jax.sharding import Mesh
from jax.sharding import PartitionSpec as P

STEP_SIZE = 0.0625
NX, NZ, NY, NC = 4, 8, 8, 2
CHIPS = NZ * NY
REGION = 16
CAP = 8
NONE = 31.0
WHOLE = (NZ * NY * 2 - 1) * REGION
WIDTH = 128
BF = jnp.bfloat16
F32 = jnp.float32
VMEM_LIMIT = 48 * 1024 * 1024


def groups_along(axes):
    ids = np.arange(NX * NZ * NY * NC).reshape(NX, NZ, NY, NC)
    size = int(np.prod([ids.shape[a] for a in axes]))
    return np.moveaxis(ids, axes, range(4 - len(axes), 4)).reshape(-1, size).tolist()


def exchange(value, axes):
    return lax.all_to_all(
        value, "d", split_axis=0, concat_axis=0, tiled=True, axis_index_groups=groups_along(axes)
    )


def of_both_cores(value):
    return lax.all_gather(value, "d", axis=0, axis_index_groups=groups_along((3,)))


def local_kernel(scale, core_ref, acts_hbm, cot_hbm, resid_hbm, count_hbm, rank_hbm,
                 resid_ref, keep_ref, give_ref,
                 acts_ref, cot_ref, acc_ref, count_ref, rank_ref, ranks_ref, chosen_ref, last_ref, pack_ref, sems):
    core = core_ref[0]
    steps, _, rows = acts_ref.shape
    cols = cot_ref.shape[2]
    tiles = cols // WIDTH
    groups = resid_ref.shape[1] // WIDTH

    copies = [
        pltpu.make_async_copy(rank_hbm, rank_ref, sems.at[0]),
        pltpu.make_async_copy(count_hbm, count_ref, sems.at[1]),
        pltpu.make_async_copy(resid_hbm, resid_ref, sems.at[2]),
    ]
    for s in range(steps):
        copies.append(pltpu.make_async_copy(acts_hbm.at[0, s], acts_ref.at[s], sems.at[3 + 2 * s]))
        copies.append(pltpu.make_async_copy(cot_hbm.at[0, s], cot_ref.at[s], sems.at[4 + 2 * s]))
    for i in [0, 1, 3, 4, 2] + list(range(5, 3 + 2 * steps)):
        copies[i].start()

    per = WIDTH // groups
    row_id = lax.broadcasted_iota(jnp.int32, (groups, WIDTH), 0)
    lane_id = lax.broadcasted_iota(jnp.int32, (groups, WIDTH), 1)
    owner_id = lax.broadcasted_iota(jnp.int32, (WIDTH, WIDTH), 0) % per
    block_id = lax.broadcasted_iota(jnp.int32, (WIDTH, WIDTH), 1) // REGION
    place = jnp.where(owner_id == block_id, 1.0, 0.0).astype(BF)
    eye = jnp.where(row_id == lane_id, 1.0, 0.0).astype(BF)
    copies[0].wait()
    copies[1].wait()
    for s in range(steps):
        for r in range(groups):
            ranks_ref[s, r:r + 1, :] = rank_ref[0, s:s + 1, r * WIDTH:(r + 1) * WIDTH]
        count = jnp.broadcast_to(count_ref[0, s:s + 1, :].astype(F32), (groups, WIDTH))
        spread = jnp.where(lane_id // per == row_id, count, 0.0)
        limit = jnp.dot(spread.astype(BF), place, preferred_element_type=F32)
        chosen = jnp.where(ranks_ref[s].astype(F32) < limit, 1.0, 0.0)
        if s == steps - 1:
            last_ref[...] = jnp.where(chosen > 0.5, ranks_ref[s].astype(F32), NONE)
        chosen_ref[s] = lax.dot_general(chosen.astype(BF), eye, (((0,), (0,)), ((), ())),
                                        preferred_element_type=F32)

    def multiply(s):
        copies[3 + 2 * s].wait()
        copies[4 + 2 * s].wait()
        left = acts_ref[s]
        half = 2 * WIDTH
        for h in range(cols // half):
            grad = lax.dot_general(left, cot_ref[s, :, h * half:(h + 1) * half],
                                   (((0,), (0,)), ((), ())), preferred_element_type=F32)
            grad = grad * scale
            for q in range(2):
                to = pl.ds(2 * h + q, rows, stride=tiles)
                acc_ref[s, to, :] = grad[:, q * WIDTH:(q + 1) * WIDTH]

    def select(s, me):
        columns = chosen_ref[s]
        for r in reversed(range(groups)):
            span = slice(r * WIDTH, (r + 1) * WIDTH)
            total = resid_ref[0, span, :] + acc_ref[s, span, :]
            mask = jnp.broadcast_to(columns[:, r:r + 1], (WIDTH, WIDTH)) > 0.5
            resid_ref[0, span, :] = jnp.where(mask, 0.0, total)
            sent = jnp.where(mask, total, 0.0).astype(BF)
            for i in range(WIDTH // REGION):
                owner = r * (WIDTH // REGION) + i
                at = ((owner // NC) * steps + s) * REGION
                tile = sent[i * REGION:(i + 1) * REGION, :]
                if owner % NC == me:
                    keep_ref[at:at + REGION, :] = tile
                elif at < WHOLE:
                    give_ref[at:at + REGION, :] = tile
                else:
                    slots = last_ref[r:r + 1, :]
                    wide = jnp.broadcast_to(slots, (REGION, WIDTH))
                    slot = lax.broadcasted_iota(jnp.int32, (REGION, WIDTH), 0).astype(F32)
                    lane = lax.broadcasted_iota(jnp.int32, (REGION, WIDTH), 1)
                    pick = jnp.where((wide == slot) & (lane // REGION == i), 1.0, 0.0)
                    packed = jnp.dot(pick.astype(BF), sent, preferred_element_type=F32)
                    pack_ref[0:CAP, :] = packed[0:CAP, :]
                    pack_ref[CAP:2 * CAP, :] = jnp.broadcast_to(slots, (CAP, WIDTH))
                    give_ref[at:at + CAP + 2, :] = pack_ref[0:CAP + 2, :].astype(BF)

    multiply(0)
    copies[2].wait()
    for me in range(NC):
        @pl.when(core == me)
        def _(me=me):
            select(0, me)
            for s in range(1, steps):
                multiply(s)
                select(s, me)


def stored_by(me, core_ref, resid_ref, store_hbm, sem):
    @pl.when(core_ref[0] == me)
    def _():
        copy = pltpu.make_async_copy(resid_ref, store_hbm, sem)
        copy.start()
        copy.wait()


def late_kernel(core_ref, after_ref, resid_ref, begun_hbm, store_hbm, sem):
    stored_by(1, core_ref, resid_ref, store_hbm, sem)


def pair_kernel(core_ref, keep_ref, both_ref, resid_ref, out_ref, store_hbm, tile_ref, sem):
    core = core_ref[0]
    other = 1 - core
    packed = both_ref[other, WHOLE:WHOLE + CAP, :].astype(F32)
    packed = jnp.concatenate([packed, jnp.zeros_like(packed)], axis=0).astype(BF)
    slots = both_ref[other, WHOLE + CAP:WHOLE + CAP + 2, :].astype(F32)[0:1, :]
    slot = lax.broadcasted_iota(jnp.int32, (REGION, WIDTH), 0).astype(F32)
    pick = jnp.where(jnp.broadcast_to(slots, (REGION, WIDTH)) == slot, 1.0, 0.0).astype(BF)
    tile_ref[...] = lax.dot_general(pick, packed, (((0,), (0,)), ((), ())), preferred_element_type=F32)
    at = pl.multiple_of(WIDTH - NC * REGION + core * REGION, REGION)
    total = keep_ref[WHOLE:WHOLE + REGION, :].astype(F32) + tile_ref[pl.ds(at, REGION), :]
    out_ref[WHOLE:WHOLE + REGION, :] = total.astype(BF)
    chunk = 8 * REGION
    for at in range(0, WHOLE, chunk):
        span = slice(at, min(at + chunk, WHOLE))
        total = keep_ref[span, :].astype(F32) + both_ref[other, span, :].astype(F32)
        out_ref[span, :] = total.astype(BF)
    stored_by(0, core_ref, resid_ref, store_hbm, sem)


def owner_kernel(arrived_ref, oresid_ref, count_ref, rank_ref, out_ref, last_ref, kept_ref):
    eye = (lax.broadcasted_iota(jnp.int32, (REGION, REGION), 0)
           == lax.broadcasted_iota(jnp.int32, (REGION, REGION), 1))
    oresid = oresid_ref[0]
    for s in range(rank_ref.shape[1]):
        total = arrived_ref[0, s].astype(F32)
        for k in range(1, arrived_ref.shape[0]):
            total = total + arrived_ref[k, s].astype(F32)
        count = jnp.broadcast_to(count_ref[0:1, s:s + 1], (1, REGION))
        row = jnp.where(rank_ref[0, s:s + 1, :] < count, 1.0, 0.0)
        square = jnp.where(eye, jnp.broadcast_to(row, (REGION, REGION)), 0.0)
        passed = jnp.broadcast_to(jnp.sum(square, axis=1, keepdims=True), (REGION, WIDTH)) > 0.5
        total = total + oresid
        going = jnp.where(passed, total, 0.0).astype(BF)
        oresid = jnp.where(passed, 0.0, total)
        for k in range(out_ref.shape[0]):
            out_ref[k, s] = going
    last_ref[...] = total
    kept_ref[...] = jnp.where(passed, 0.0, 1.0)


def update_kernel(arrived_ref, out_ref):
    total = jnp.zeros((REGION, WIDTH), F32)
    for s in range(arrived_ref.shape[1]):
        cross = arrived_ref[0, s].astype(F32)
        for x in range(1, NX):
            cross = cross + arrived_ref[x, s].astype(F32)
        total = total + cross.astype(BF).astype(F32)
    applied = (-STEP_SIZE * total).astype(BF)
    for k in range(out_ref.shape[0]):
        out_ref[k] = applied


def assemble_kernel(halves_ref, last_ref, kept_ref, out_ref, oresid_ref, flat_ref):
    oresid_ref[0] = jnp.where(kept_ref[...] > 0.5, last_ref[...], 0.0)
    rows, cols = out_ref.shape
    tiles = cols // WIDTH
    for i in range(CHIPS):
        for c in range(NC):
            at = (i * NC + c) * REGION
            flat_ref[at:at + REGION, :] = halves_ref[c, i].astype(F32)
    for t in range(tiles):
        out_ref[:, t * WIDTH:(t + 1) * WIDTH] = flat_ref[pl.ds(t, rows, stride=tiles), :].astype(BF)


def vmem():
    return pl.BlockSpec(memory_space=pltpu.VMEM)


def hbm():
    return pl.BlockSpec(memory_space=pltpu.HBM)


def smem():
    return pl.BlockSpec(memory_space=pltpu.SMEM)


def per_device(acts, cotangent, residual, owner_residual, in_count, in_rank, out_count, out_rank):
    steps, tokens, rows = acts.shape[1:]
    cols = cotangent.shape[3]
    blocks = residual.shape[1]
    scale = 1.0 / math.sqrt(tokens * CHIPS * NC)
    core = (lax.axis_index("d") % NC).astype(jnp.int32).reshape(1)
    params = pltpu.CompilerParams(vmem_limit_bytes=VMEM_LIMIT)

    def local(*args):
        return local_kernel(scale, *args)

    size = CHIPS * steps * REGION
    new_resid, keep, give = pl.pallas_call(
        local,
        in_specs=[smem(), hbm(), hbm(), hbm(), hbm(), hbm()],
        out_specs=[vmem(), vmem(), vmem()],
        out_shape=[
            pltpu.VMEM(residual.shape, F32),
            jax.ShapeDtypeStruct((size, WIDTH), BF),
            jax.ShapeDtypeStruct((WHOLE + CAP + 2, WIDTH), BF),
        ],
        scratch_shapes=[
            pltpu.VMEM((steps, tokens, rows), BF),
            pltpu.VMEM((steps, tokens, cols), BF),
            pltpu.VMEM((steps, blocks, WIDTH), F32),
            pltpu.VMEM(in_count.shape, jnp.int32),
            pltpu.VMEM(in_rank.shape, jnp.int32),
            pltpu.VMEM((steps, blocks // WIDTH, WIDTH), jnp.int32),
            pltpu.VMEM((steps, WIDTH, WIDTH), F32),
            pltpu.VMEM((blocks // WIDTH, WIDTH), F32),
            pltpu.VMEM((2 * CAP, WIDTH), F32),
            pltpu.SemaphoreType.DMA((3 + 2 * steps,)),
        ],
        compiler_params=params,
        name="local",
    )(core, *[pltpu.with_memory_space_constraint(v, pltpu.HBM)
            for v in (acts, cotangent, residual, in_count, in_rank)])

    placed = jax.ShapeDtypeStruct(residual.shape, F32)
    pair, store = pl.pallas_call(
        pair_kernel,
        in_specs=[smem(), vmem(), vmem(), vmem()],
        out_specs=[vmem(), hbm()],
        out_shape=[jax.ShapeDtypeStruct((size, WIDTH), BF), placed],
        scratch_shapes=[pltpu.VMEM((WIDTH, WIDTH), F32), pltpu.SemaphoreType.DMA],
        compiler_params=params,
        name="pair",
    )(core, keep, of_both_cores(give), new_resid)
    pair = pair.reshape(CHIPS, steps, REGION, WIDTH)
    arrived = exchange(pair, (1, 2))

    tile = jax.ShapeDtypeStruct((REGION, WIDTH), F32)
    outgoing, last, kept = pl.pallas_call(
        owner_kernel,
        in_specs=[vmem(), vmem(), vmem(), vmem()],
        out_specs=[vmem(), vmem(), vmem()],
        out_shape=[jax.ShapeDtypeStruct((NX, steps, REGION, WIDTH), BF), tile, tile],
        compiler_params=params,
        name="owner",
    )(arrived, owner_residual, out_count, out_rank)

    copies = pl.pallas_call(
        update_kernel,
        in_specs=[vmem()],
        out_specs=vmem(),
        out_shape=jax.ShapeDtypeStruct((CHIPS, REGION, WIDTH), BF),
        compiler_params=params,
        name="update",
    )(exchange(outgoing, (0,)))
    own = exchange(copies, (1, 2))
    new_residual = pl.pallas_call(
        late_kernel,
        in_specs=[smem(), pl.BlockSpec(memory_space=pl.ANY), vmem(), hbm()],
        out_specs=hbm(),
        out_shape=placed,
        scratch_shapes=[pltpu.SemaphoreType.DMA],
        input_output_aliases={3: 0},
        compiler_params=params,
        name="late",
    )(core, own, new_resid, store)
    own, new_residual = lax.optimization_barrier((own, new_residual))
    halves = of_both_cores(own)
    applied, new_owner = pl.pallas_call(
        assemble_kernel,
        in_specs=[vmem(), vmem(), vmem()],
        out_specs=[vmem(), vmem()],
        out_shape=[
            jax.ShapeDtypeStruct((rows, cols), BF),
            jax.ShapeDtypeStruct(owner_residual.shape, F32),
        ],
        scratch_shapes=[
            pltpu.VMEM((blocks, WIDTH), F32),
        ],
        compiler_params=params,
        name="assemble",
    )(halves, last, kept)
    return applied, new_residual, new_owner


def solution(mesh):
    flat = Mesh(mesh.devices.reshape(-1), ("d",))
    spec = P("d")
    return jax.shard_map(
        per_device,
        mesh=flat,
        in_specs=(spec,) * 8,
        out_specs=(P(), spec, spec),
        check_vma=False,
    )
```

```python
import math

import jax
import jax.numpy as jnp
import numpy as np
from jax import lax
from jax.experimental import pallas as pl
from jax.experimental.pallas import tpu as pltpu
from jax.sharding import Mesh
from jax.sharding import PartitionSpec as P

STEP_SIZE = 0.0625
NX, NZ, NY, NC = 4, 8, 8, 2
CHIPS = NZ * NY
REGION = 16
CAP = 8
NONE = 31.0
WHOLE = (NZ * NY * 2 - 1) * REGION
WIDTH = 128
BF = jnp.bfloat16
F32 = jnp.float32
VMEM_LIMIT = 48 * 1024 * 1024


def groups_along(axes):
    ids = np.arange(NX * NZ * NY * NC).reshape(NX, NZ, NY, NC)
    size = int(np.prod([ids.shape[a] for a in axes]))
    return np.moveaxis(ids, axes, range(4 - len(axes), 4)).reshape(-1, size).tolist()


def exchange(value, axes):
    return lax.all_to_all(
        value, "d", split_axis=0, concat_axis=0, tiled=True, axis_index_groups=groups_along(axes)
    )


def of_both_cores(value):
    return lax.all_gather(value, "d", axis=0, axis_index_groups=groups_along((3,)))


def local_kernel(scale, core_ref, acts_hbm, cot_hbm, resid_hbm, count_hbm, rank_hbm,
                 resid_ref, keep_ref, give_ref,
                 acts_ref, cot_ref, acc_ref, count_ref, rank_ref, ranks_ref, chosen_ref, last_ref, pack_ref, sems):
    core = core_ref[0]
    steps, _, rows = acts_ref.shape
    cols = cot_ref.shape[2]
    tiles = cols // WIDTH
    groups = resid_ref.shape[1] // WIDTH

    copies = [
        pltpu.make_async_copy(rank_hbm, rank_ref, sems.at[0]),
        pltpu.make_async_copy(count_hbm, count_ref, sems.at[1]),
        pltpu.make_async_copy(resid_hbm, resid_ref, sems.at[2]),
    ]
    for s in range(steps):
        copies.append(pltpu.make_async_copy(acts_hbm.at[0, s], acts_ref.at[s], sems.at[3 + 2 * s]))
        copies.append(pltpu.make_async_copy(cot_hbm.at[0, s], cot_ref.at[s], sems.at[4 + 2 * s]))
    for i in [0, 1, 3, 4, 2] + list(range(5, 3 + 2 * steps)):
        copies[i].start()

    per = WIDTH // groups
    row_id = lax.broadcasted_iota(jnp.int32, (groups, WIDTH), 0)
    lane_id = lax.broadcasted_iota(jnp.int32, (groups, WIDTH), 1)
    owner_id = lax.broadcasted_iota(jnp.int32, (WIDTH, WIDTH), 0) % per
    block_id = lax.broadcasted_iota(jnp.int32, (WIDTH, WIDTH), 1) // REGION
    place = jnp.where(owner_id == block_id, 1.0, 0.0).astype(BF)
    eye = jnp.where(row_id == lane_id, 1.0, 0.0).astype(BF)
    copies[0].wait()
    copies[1].wait()
    for s in range(steps):
        for r in range(groups):
            ranks_ref[s, r:r + 1, :] = rank_ref[0, s:s + 1, r * WIDTH:(r + 1) * WIDTH]
        count = jnp.broadcast_to(count_ref[0, s:s + 1, :].astype(F32), (groups, WIDTH))
        spread = jnp.where(lane_id // per == row_id, count, 0.0)
        limit = jnp.dot(spread.astype(BF), place, preferred_element_type=F32)
        chosen = jnp.where(ranks_ref[s].astype(F32) < limit, 1.0, 0.0)
        if s == steps - 1:
            last_ref[...] = jnp.where(chosen > 0.5, ranks_ref[s].astype(F32), NONE)
        chosen_ref[s] = lax.dot_general(chosen.astype(BF), eye, (((0,), (0,)), ((), ())),
                                        preferred_element_type=F32)

    def multiply(s):
        copies[3 + 2 * s].wait()
        copies[4 + 2 * s].wait()
        left = acts_ref[s]
        half = 2 * WIDTH
        for h in range(cols // half):
            grad = lax.dot_general(left, cot_ref[s, :, h * half:(h + 1) * half],
                                   (((0,), (0,)), ((), ())), preferred_element_type=F32)
            grad = grad * scale
            for q in range(2):
                to = pl.ds(2 * h + q, rows, stride=tiles)
                acc_ref[s, to, :] = grad[:, q * WIDTH:(q + 1) * WIDTH]

    def select(s, me):
        columns = chosen_ref[s]
        for r in reversed(range(groups)):
            span = slice(r * WIDTH, (r + 1) * WIDTH)
            total = resid_ref[0, span, :] + acc_ref[s, span, :]
            mask = jnp.broadcast_to(columns[:, r:r + 1], (WIDTH, WIDTH)) > 0.5
            resid_ref[0, span, :] = jnp.where(mask, 0.0, total)
            sent = jnp.where(mask, total, 0.0).astype(BF)
            for i in range(WIDTH // REGION):
                owner = r * (WIDTH // REGION) + i
                at = ((owner // NC) * steps + s) * REGION
                tile = sent[i * REGION:(i + 1) * REGION, :]
                if owner % NC == me:
                    keep_ref[at:at + REGION, :] = tile
                elif at < WHOLE:
                    give_ref[at:at + REGION, :] = tile
                else:
                    slots = last_ref[r:r + 1, :]
                    wide = jnp.broadcast_to(slots, (REGION, WIDTH))
                    slot = lax.broadcasted_iota(jnp.int32, (REGION, WIDTH), 0).astype(F32)
                    lane = lax.broadcasted_iota(jnp.int32, (REGION, WIDTH), 1)
                    pick = jnp.where((wide == slot) & (lane // REGION == i), 1.0, 0.0)
                    packed = jnp.dot(pick.astype(BF), sent, preferred_element_type=F32)
                    pack_ref[0:CAP, :] = packed[0:CAP, :]
                    pack_ref[CAP:2 * CAP, :] = jnp.broadcast_to(slots, (CAP, WIDTH))
                    give_ref[at:at + CAP + 2, :] = pack_ref[0:CAP + 2, :].astype(BF)

    multiply(0)
    copies[2].wait()
    for me in range(NC):
        @pl.when(core == me)
        def _(me=me):
            select(0, me)
            for s in range(1, steps):
                multiply(s)
                select(s, me)


def stored_by(me, core_ref, resid_ref, store_hbm, sem):
    @pl.when(core_ref[0] == me)
    def _():
        copy = pltpu.make_async_copy(resid_ref, store_hbm, sem)
        copy.start()
        copy.wait()


def late_kernel(core_ref, after_ref, resid_ref, begun_hbm, store_hbm, sem):
    stored_by(1, core_ref, resid_ref, store_hbm, sem)


def pair_kernel(core_ref, keep_ref, both_ref, resid_ref, out_ref, store_hbm, tile_ref, sem):
    core = core_ref[0]
    other = 1 - core
    packed = both_ref[other, WHOLE:WHOLE + CAP, :].astype(F32)
    packed = jnp.concatenate([packed, jnp.zeros_like(packed)], axis=0).astype(BF)
    slots = both_ref[other, WHOLE + CAP:WHOLE + CAP + 2, :].astype(F32)[0:1, :]
    slot = lax.broadcasted_iota(jnp.int32, (REGION, WIDTH), 0).astype(F32)
    pick = jnp.where(jnp.broadcast_to(slots, (REGION, WIDTH)) == slot, 1.0, 0.0).astype(BF)
    tile_ref[...] = lax.dot_general(pick, packed, (((0,), (0,)), ((), ())), preferred_element_type=F32)
    at = pl.multiple_of(WIDTH - NC * REGION + core * REGION, REGION)
    total = keep_ref[WHOLE:WHOLE + REGION, :].astype(F32) + tile_ref[pl.ds(at, REGION), :]
    out_ref[WHOLE:WHOLE + REGION, :] = total.astype(BF)
    chunk = 8 * REGION
    for at in range(0, WHOLE, chunk):
        span = slice(at, min(at + chunk, WHOLE))
        out_ref[span, :] = keep_ref[span, :] + both_ref[other, span, :]
    stored_by(0, core_ref, resid_ref, store_hbm, sem)


def owner_kernel(arrived_ref, oresid_ref, count_ref, rank_ref, out_ref, last_ref, kept_ref):
    eye = (lax.broadcasted_iota(jnp.int32, (REGION, REGION), 0)
           == lax.broadcasted_iota(jnp.int32, (REGION, REGION), 1))
    oresid = oresid_ref[0]
    for s in range(rank_ref.shape[1]):
        total = arrived_ref[0, s].astype(F32)
        for k in range(1, arrived_ref.shape[0]):
            total = total + arrived_ref[k, s].astype(F32)
        count = jnp.broadcast_to(count_ref[0:1, s:s + 1], (1, REGION))
        row = jnp.where(rank_ref[0, s:s + 1, :] < count, 1.0, 0.0)
        square = jnp.where(eye, jnp.broadcast_to(row, (REGION, REGION)), 0.0)
        passed = jnp.broadcast_to(jnp.sum(square, axis=1, keepdims=True), (REGION, WIDTH)) > 0.5
        total = total + oresid
        going = jnp.where(passed, total, 0.0).astype(BF)
        oresid = jnp.where(passed, 0.0, total)
        for k in range(out_ref.shape[0]):
            out_ref[k, s] = going
    last_ref[...] = total
    kept_ref[...] = jnp.where(passed, 0.0, 1.0)


def update_kernel(arrived_ref, out_ref):
    total = jnp.zeros((REGION, WIDTH), F32)
    for s in range(arrived_ref.shape[1]):
        cross = arrived_ref[0, s].astype(F32)
        for x in range(1, NX):
            cross = cross + arrived_ref[x, s].astype(F32)
        total = total + cross.astype(BF).astype(F32)
    applied = (-STEP_SIZE * total).astype(BF)
    for k in range(out_ref.shape[0]):
        out_ref[k] = applied


def assemble_kernel(halves_ref, last_ref, kept_ref, out_ref, oresid_ref, flat_ref):
    oresid_ref[0] = jnp.where(kept_ref[...] > 0.5, last_ref[...], 0.0)
    rows, cols = out_ref.shape
    tiles = cols // WIDTH
    for i in range(CHIPS):
        for c in range(NC):
            at = (i * NC + c) * REGION
            flat_ref[at:at + REGION, :] = halves_ref[c, i].astype(F32)
    for t in range(tiles):
        out_ref[:, t * WIDTH:(t + 1) * WIDTH] = flat_ref[pl.ds(t, rows, stride=tiles), :].astype(BF)


def vmem():
    return pl.BlockSpec(memory_space=pltpu.VMEM)


def hbm():
    return pl.BlockSpec(memory_space=pltpu.HBM)


def smem():
    return pl.BlockSpec(memory_space=pltpu.SMEM)


def per_device(acts, cotangent, residual, owner_residual, in_count, in_rank, out_count, out_rank):
    steps, tokens, rows = acts.shape[1:]
    cols = cotangent.shape[3]
    blocks = residual.shape[1]
    scale = 1.0 / math.sqrt(tokens * CHIPS * NC)
    core = (lax.axis_index("d") % NC).astype(jnp.int32).reshape(1)
    params = pltpu.CompilerParams(vmem_limit_bytes=VMEM_LIMIT)

    def local(*args):
        return local_kernel(scale, *args)

    size = CHIPS * steps * REGION
    new_resid, keep, give = pl.pallas_call(
        local,
        in_specs=[smem(), hbm(), hbm(), hbm(), hbm(), hbm()],
        out_specs=[vmem(), vmem(), vmem()],
        out_shape=[
            pltpu.VMEM(residual.shape, F32),
            jax.ShapeDtypeStruct((size, WIDTH), BF),
            jax.ShapeDtypeStruct((WHOLE + CAP + 2, WIDTH), BF),
        ],
        scratch_shapes=[
            pltpu.VMEM((steps, tokens, rows), BF),
            pltpu.VMEM((steps, tokens, cols), BF),
            pltpu.VMEM((steps, blocks, WIDTH), F32),
            pltpu.VMEM(in_count.shape, jnp.int32),
            pltpu.VMEM(in_rank.shape, jnp.int32),
            pltpu.VMEM((steps, blocks // WIDTH, WIDTH), jnp.int32),
            pltpu.VMEM((steps, WIDTH, WIDTH), F32),
            pltpu.VMEM((blocks // WIDTH, WIDTH), F32),
            pltpu.VMEM((2 * CAP, WIDTH), F32),
            pltpu.SemaphoreType.DMA((3 + 2 * steps,)),
        ],
        compiler_params=params,
        name="local",
    )(core, *[pltpu.with_memory_space_constraint(v, pltpu.HBM)
            for v in (acts, cotangent, residual, in_count, in_rank)])

    placed = jax.ShapeDtypeStruct(residual.shape, F32)
    pair, store = pl.pallas_call(
        pair_kernel,
        in_specs=[smem(), vmem(), vmem(), vmem()],
        out_specs=[vmem(), hbm()],
        out_shape=[jax.ShapeDtypeStruct((size, WIDTH), BF), placed],
        scratch_shapes=[pltpu.VMEM((WIDTH, WIDTH), F32), pltpu.SemaphoreType.DMA],
        compiler_params=params,
        name="pair",
    )(core, keep, of_both_cores(give), new_resid)
    pair = pair.reshape(CHIPS, steps, REGION, WIDTH)
    arrived = exchange(pair, (1, 2))

    tile = jax.ShapeDtypeStruct((REGION, WIDTH), F32)
    outgoing, last, kept = pl.pallas_call(
        owner_kernel,
        in_specs=[vmem(), vmem(), vmem(), vmem()],
        out_specs=[vmem(), vmem(), vmem()],
        out_shape=[jax.ShapeDtypeStruct((NX, steps, REGION, WIDTH), BF), tile, tile],
        compiler_params=params,
        name="owner",
    )(arrived, owner_residual, out_count, out_rank)

    copies = pl.pallas_call(
        update_kernel,
        in_specs=[vmem()],
        out_specs=vmem(),
        out_shape=jax.ShapeDtypeStruct((CHIPS, REGION, WIDTH), BF),
        compiler_params=params,
        name="update",
    )(exchange(outgoing, (0,)))
    own = exchange(copies, (1, 2))
    new_residual = pl.pallas_call(
        late_kernel,
        in_specs=[smem(), pl.BlockSpec(memory_space=pl.ANY), vmem(), hbm()],
        out_specs=hbm(),
        out_shape=placed,
        scratch_shapes=[pltpu.SemaphoreType.DMA],
        input_output_aliases={3: 0},
        compiler_params=params,
        name="late",
    )(core, own, new_resid, store)
    own, new_residual = lax.optimization_barrier((own, new_residual))
    halves = of_both_cores(own)
    applied, new_owner = pl.pallas_call(
        assemble_kernel,
        in_specs=[vmem(), vmem(), vmem()],
        out_specs=[vmem(), vmem()],
        out_shape=[
            jax.ShapeDtypeStruct((rows, cols), BF),
            jax.ShapeDtypeStruct(owner_residual.shape, F32),
        ],
        scratch_shapes=[
            pltpu.VMEM((blocks, WIDTH), F32),
        ],
        compiler_params=params,
        name="assemble",
    )(halves, last, kept)
    return applied, new_residual, new_owner


def solution(mesh):
    flat = Mesh(mesh.devices.reshape(-1), ("d",))
    spec = P("d")
    return jax.shard_map(
        per_device,
        mesh=flat,
        in_specs=(spec,) * 8,
        out_specs=(P(), spec, spec),
        check_vma=False,
    )
```
